32 devices in a mesh: bytes: 4 (over z), ctx: 2 (over x), tp: 4 (over y, core).
Axes of the slice: x: 2, y: 2, z: 4, core: 2. Of those that a mesh axis runs over, the one named last changes fastest.
Arguments:
- byte_values_sequence: int32 [1536], P(('bytes', 'ctx')), may hold values from 0 to 255
- offsets: int32 [1536], P(('bytes', 'ctx')), may hold values from 0 to 168, as said below
- byte_table: bfloat16 [256, 1024], replicated, may hold values from -6 to 6
- byte_query: bfloat16 [1024, 1024], P(None, 'tp'), may hold values from -1 to 1
- byte_key: bfloat16 [1024, 1024], P(None, 'tp'), may hold values from -16 to 16
- byte_value: bfloat16 [1024, 1024], P(None, 'tp'), may hold values from -0.1875 to 0.1875
- latent_query: bfloat16 [1024, 4096], P(None, ('ctx', 'tp')), may hold values from -1 to 1
- latent_key: bfloat16 [1024, 4096], P(None, ('ctx', 'tp')), may hold values from -16 to 16
- latent_value: bfloat16 [1024, 4096], P(None, ('ctx', 'tp')), may hold values from -0.1875 to 0.1875
- decode_weight: bfloat16 [4096, 1024], P(('ctx', 'tp')), may hold values from -0.75 to 0.75
Outputs:
- byte_output: bfloat16 [1536, 1024], P(('bytes', 'ctx'), 'tp')
The draws below stay inside these ranges and needn't reach their ends.
Inputs may be any that keep to these rules, and one draw needn't show every extreme that they name: offsets[i] is 0 where a patch starts and offsets[i - 1] + 1 elsewhere; the first byte of every device's 192 bytes starts a patch; one device's bytes hold 24 to 72 patch starts and the bytes of the devices of one index of bytes hold at most 96; both most values are reached in every draw.
All inputs are finite; a program needn't handle non-finite values.
Results may differ from the reference program's by a relative error of at most 0.017.
Values may be sent and summed in bfloat16 or wider, within the bound.
A program may use at most 64 MiB of HBM per device.

```python
import math
import jax
import jax.numpy as jnp
import numpy as np
from jax import lax

BYTES_DEV = 192
DB = 1024
HEADS_B = 16
HEADS_L = 32
HEAD_L = 128
VOCAB = 256
BLOCKS = 8
SEQ = 1536
PCAP = 72
GCAP = 96
PATCHES = 384


def draw_offsets(key, part):
    per_group = GCAP * 4 // BYTES_DEV
    groups = BLOCKS // per_group
    lowest = BYTES_DEV // 8
    headroom = PCAP - lowest
    budget = GCAP - per_group * lowest
    key_surplus, key_group, key_places = jax.random.split(key, 3)
    key_sparse = jax.random.fold_in(key, 29)
    surplus = jax.random.randint(key_surplus, (groups, per_group), 0, headroom + 1, dtype=jnp.int32)
    forced = jax.random.randint(key_group, (), 0, groups, dtype=jnp.int32)
    sparse_group = jax.random.randint(key_sparse, (), 0, groups, dtype=jnp.int32)
    surplus = jnp.where((jnp.arange(groups, dtype=jnp.int32) == forced)[:, None], headroom, surplus)
    sparse_cell = (jnp.arange(groups, dtype=jnp.int32) == sparse_group)[:, None] & (jnp.arange(per_group, dtype=jnp.int32) == per_group - 1)[None, :]
    surplus = jnp.where(sparse_cell, 0, surplus)
    capped = jnp.minimum(jnp.cumsum(surplus, axis=1), budget)
    surplus = capped - jnp.concatenate([jnp.zeros((groups, 1), jnp.int32), capped[:, :-1]], axis=1)
    counts = (lowest + surplus).reshape(BLOCKS)
    places = jnp.arange(BYTES_DEV, dtype=jnp.int32)
    attention_scores = jax.random.randint(key_places, (BLOCKS, BYTES_DEV), 1, 1 << 20, dtype=jnp.int32) * BYTES_DEV + places[None, :]
    sparse_block = sparse_group * per_group + per_group - 1
    is_sparse = (jnp.arange(BLOCKS, dtype=jnp.int32) == sparse_block)[:, None]
    tail_scores = jnp.where(places >= BYTES_DEV - lowest + 1, places, (1 << 20) * BYTES_DEV + places)
    attention_scores = jnp.where(is_sparse, tail_scores[None, :], attention_scores)
    attention_scores = jnp.where(places[None, :] == 0, 0, attention_scores)
    ranking = jnp.argsort(jnp.argsort(attention_scores, axis=1, stable=True), axis=1, stable=True)
    starts = (ranking < counts[:, None]).reshape(SEQ)
    indices = jnp.arange(SEQ, dtype=jnp.int32)
    latest = lax.cummax(jnp.where(starts, indices, 0), axis=0)
    return (indices - latest).astype(jnp.int32)


def paired(key, salt_value, fan_in, head_count, head_feature_width):
    query_key_product, key_other = jax.random.split(jax.random.fold_in(key, salt_value), 2)
    dimensions = (fan_in, head_count * head_feature_width)
    queries = jnp.clip(jax.random.normal(query_key_product, dimensions, jnp.float32) * fan_in ** (-0.5), -1.0, 1.0)
    key_side = jax.random.normal(key_other, dimensions, jnp.float32) * fan_in ** (-0.5)
    return (queries, jnp.clip(key_side, -16.0, 16.0))


def draw_byte_query(key, part):
    return paired(key, 11, DB, HEADS_B, DB // HEADS_B)[0].astype(jnp.bfloat16)


def draw_byte_key(key, part):
    return paired(key, 11, DB, HEADS_B, DB // HEADS_B)[1].astype(jnp.bfloat16)


def draw_latent_query(key, part):
    return paired(key, 13, DB, HEADS_L, HEAD_L)[0].astype(jnp.bfloat16)


def draw_latent_key(key, part):
    return paired(key, 13, DB, HEADS_L, HEAD_L)[1].astype(jnp.bfloat16)


def touch_ends(values, stream_key, least, largest):
    dims = values.shape
    place = [jax.random.randint(jax.random.fold_in(stream_key, axis), (), 0, dims[axis]) for axis in range(len(dims))]
    values = values.at[tuple(place)].set(least)
    longest = dims.index(max(dims))
    place[longest] = (place[longest] + 1) % dims[longest]
    return values.at[tuple(place)].set(largest)


def spiked(result, rng, source, target, blocks, factor):
    def block_of(axis_at):
        return (jnp.arange(result.shape[axis_at]) // (result.shape[axis_at] // blocks)).reshape((-1,) + (1,) * (result.ndim - 1 - axis_at))

    first = jax.random.permutation(rng, blocks)[block_of(target)]
    second = (block_of(target) + blocks // 2) % blocks
    return jnp.where((block_of(source) == first) | (block_of(source) == second), factor * result, result)


def block_levels(stream_key, shape, shards, least, high):
    factor_of, own = 1.0, jax.random.fold_in(stream_key, 6)
    for dim, blocks in shards:
        steps = jnp.exp(jax.random.uniform(jax.random.fold_in(own, dim), (blocks,), jnp.float32, least / len(shards), high / len(shards)))
        factor_of = factor_of * jnp.repeat(steps, shape[dim] // blocks).reshape([-1 if axis == dim else 1 for axis in range(len(shape))])
    return factor_of


def rank_bounds(count, skew):
    portions = [(1 << 20) // math.isqrt(grade ** skew) + 1 for grade in range(1, count + 1)]
    scale = 1 + sum(portions) // (1 << 30)
    return np.cumsum(np.array([max(1, weight // scale) for weight in portions]))


def skewed_ids(stream_key, extent, amount, slope):
    listing = rank_bounds(amount, slope)
    ticket = jax.random.randint(jax.random.fold_in(stream_key, 1), extent, 0, int(listing[amount - 1]))
    standing = jnp.searchsorted(jnp.asarray(listing, jnp.int32), ticket, side="right")
    return jax.random.permutation(jax.random.fold_in(stream_key, 2), amount)[standing].astype(jnp.int32)


def noise(stream_key, shape, scale, bound, shards=(), held_as=jnp.bfloat16):
    gain = block_levels(stream_key, shape, shards, -0.22, 0.18) if shards else 1.0
    drawn = jax.random.normal(stream_key, shape, jnp.float32) * scale * gain
    return jnp.minimum(jnp.maximum(drawn, -bound), bound).astype(held_as)


def bell_draw_with(stream_key, shape, scale, most, cuts, heavy, kind=jnp.bfloat16):
    drawn = scale * jax.random.normal(stream_key, shape, jnp.float32)
    if cuts:
        drawn = drawn * block_levels(stream_key, shape, cuts, -0.22, 0.18)
    return jnp.clip(spiked(drawn, jax.random.fold_in(stream_key, 3), *heavy), -most, most).astype(kind)


def setup_inputs(seed: int = 0) -> dict:
    streams_of = jax.random.split(jax.random.key(seed), 11)
    return {
        "byte_values_sequence": touch_ends(skewed_ids(streams_of[0], (SEQ,), VOCAB, 2), jax.random.fold_in(streams_of[0], 3), 0, VOCAB - 1).astype(jnp.int32),
        "offsets": draw_offsets(jax.random.fold_in(streams_of[10], 71), 0),
        "byte_table": noise(streams_of[2], (VOCAB, DB), 1.0, 6.0),
        "byte_query": draw_byte_query(jax.random.fold_in(streams_of[10], 71), 0),
        "byte_key": draw_byte_key(jax.random.fold_in(streams_of[10], 71), 0),
        "byte_value": noise(streams_of[5], (DB, DB), DB ** -0.5, 0.1875, ((1, 4),)),
        "latent_query": draw_latent_query(jax.random.fold_in(streams_of[10], 71), 0),
        "latent_key": draw_latent_key(jax.random.fold_in(streams_of[10], 71), 0),
        "latent_value": noise(streams_of[8], (DB, HEADS_L * HEAD_L), DB ** -0.5, 0.1875, ((1, 8),)),
        "decode_weight": bell_draw_with(streams_of[9], (HEADS_L * HEAD_L, DB), HEAD_L ** -0.5, 0.75, ((0, 8),), (0, 1, 8, 2.0)),
    }


EPSILON = 1e-06
NEGATIVE = -1e+30

def norm_rows(values):
    values = values.astype(jnp.float32)
    return values * lax.rsqrt(lax.optimization_barrier(jnp.mean(values * values, axis=-1, keepdims=True)) + EPSILON)

def rounded(values):
    return lax.optimization_barrier(values.astype(jnp.bfloat16)).astype(jnp.float32)

def project(inputs, weight):
    return jnp.dot(inputs, weight, preferred_element_type=jnp.float32).astype(jnp.bfloat16)

def softmax_mix(attention_scores, allowed, values):
    attention_scores = jnp.where(allowed, attention_scores, NEGATIVE)
    highest = lax.optimization_barrier(jnp.max(attention_scores, axis=-1, keepdims=True))
    weights = jnp.where(allowed, jnp.exp(attention_scores - highest), 0.0)
    totals = lax.optimization_barrier(jnp.sum(weights, axis=-1, keepdims=True))
    blended = jnp.einsum('...qk,...kd->...qd', rounded(weights), values, precision=lax.Precision.HIGHEST)
    return blended / totals

def reference(byte_values_sequence, offsets, byte_table, byte_query, byte_key, byte_value, latent_query, latent_key, latent_value, decode_weight):
    head_feature_width = DB // HEADS_B
    block_count = SEQ // BYTES_DEV
    normed = norm_rows(byte_table[byte_values_sequence]).astype(jnp.bfloat16)
    byte_window_queries = project(normed, byte_query)
    byte_window_keys = project(normed, byte_key)
    values_b = project(normed, byte_value)
    query_pos = jnp.arange(BYTES_DEV, dtype=jnp.int32)[:, None]
    key_pos = jnp.arange(2 * BYTES_DEV, dtype=jnp.int32)[None, :]
    inside = (key_pos > query_pos) & (key_pos <= query_pos + BYTES_DEV)
    opening = (jnp.arange(block_count, dtype=jnp.int32) == 0)[:, None, None] & (key_pos < BYTES_DEV)[None]
    allowed_b = inside[None] & jnp.logical_not(opening)

    def keys_with_earlier(blocks):
        earlier = jnp.concatenate([jnp.zeros_like(blocks[:1]), blocks[:-1]], axis=0)
        return jnp.concatenate([earlier, blocks], axis=1)

    def byte_head(head_index):

        def column_positions(values):
            picked = lax.dynamic_slice_in_dim(values, head_index * head_feature_width, head_feature_width, 1)
            return picked.astype(jnp.float32).reshape(block_count, BYTES_DEV, head_feature_width)
        attention_scores = jnp.einsum('gye,gje->gyj', column_positions(byte_window_queries), keys_with_earlier(column_positions(byte_window_keys)), precision=lax.Precision.HIGHEST) / math.sqrt(head_feature_width)
        blended = softmax_mix(attention_scores, allowed_b, keys_with_earlier(column_positions(values_b)))
        return blended.reshape(SEQ, head_feature_width)
    encoded = lax.map(byte_head, jnp.arange(HEADS_B, dtype=jnp.int32))
    encoded = encoded.transpose(1, 0, 2).reshape(SEQ, DB).astype(jnp.bfloat16)
    patch_of = jnp.cumsum((offsets == 0).astype(jnp.int32)) - 1
    lengths = jax.ops.segment_sum(jnp.ones((SEQ,), jnp.float32), patch_of, num_segments=PATCHES)
    patch_sums = jax.ops.segment_sum(encoded.astype(jnp.float32), patch_of, num_segments=PATCHES)
    pooled = (patch_sums / jnp.maximum(lengths, 1.0)[:, None]).astype(jnp.bfloat16)
    latent_in = norm_rows(pooled).astype(jnp.bfloat16)
    patch_ids = jnp.arange(PATCHES, dtype=jnp.int32)
    present = patch_ids <= patch_of[-1]
    queries_l = project(latent_in, latent_query)
    keys_l = project(latent_in, latent_key)
    values_l = project(latent_in, latent_value)
    block_rows = math.gcd(PATCHES, 512)

    def latent_head(head_index):

        def column_positions(values):
            return lax.dynamic_slice_in_dim(values, head_index * HEAD_L, HEAD_L, 1).astype(jnp.float32)
        queries_h = column_positions(queries_l)
        keys_h = column_positions(keys_l)
        values_h = column_positions(values_l)

        def query_block(block_index):
            picked = lax.dynamic_slice_in_dim(queries_h, block_index * block_rows, block_rows, 0)
            ordinals = block_index * block_rows + jnp.arange(block_rows, dtype=jnp.int32)
            allowed = (patch_ids[None, :] <= ordinals[:, None]) & present[None, :]
            attention_scores = jnp.dot(picked, keys_h.T, precision=lax.Precision.HIGHEST) / math.sqrt(HEAD_L)
            return softmax_mix(attention_scores, allowed, values_h)
        blended = lax.map(query_block, jnp.arange(PATCHES // block_rows, dtype=jnp.int32))
        return blended.reshape(PATCHES, HEAD_L)
    latent_out = lax.map(latent_head, jnp.arange(HEADS_L, dtype=jnp.int32))
    latent_out = latent_out.transpose(1, 0, 2).reshape(PATCHES, HEADS_L * HEAD_L).astype(jnp.bfloat16)
    decoded = jnp.dot(latent_out, decode_weight, preferred_element_type=jnp.float32)
    return (encoded.astype(jnp.float32) + decoded[patch_of]).astype(jnp.bfloat16)
```

```python
import functools
import math

import jax
import jax.numpy as jnp
from jax import lax
from jax.experimental import pallas as pl
from jax.experimental.pallas import tpu as pltpu
from jax.sharding import PartitionSpec as P

DB = 1024
HEADS_B = 16
HEAD_L = 128


EPSILON = 1e-06
NEGATIVE = -1e30
FARAWAY = 1 << 30


def from_behind(value, axis, steps):
    count = lax.axis_size(axis)
    first, last = (max(0, -steps), min(count, count - steps))
    return lax.ppermute(value, axis, [(source, source + steps) for source in range(first, last)])


def norm_rows(values):
    values = values.astype(jnp.float32)
    return values * lax.rsqrt(jnp.mean(values * values, axis=-1, keepdims=True) + EPSILON)


def project(inputs, weight):
    return jnp.dot(inputs, weight, preferred_element_type=jnp.float32).astype(jnp.bfloat16)


def byte_project(byte_values_sequence, byte_table, weights):
    onehot = (
        byte_values_sequence[:, None] == jnp.arange(byte_table.shape[0], dtype=jnp.int32)[None, :]
    ).astype(jnp.bfloat16)
    embedded = jnp.dot(onehot, byte_table, preferred_element_type=jnp.float32)
    normed = norm_rows(embedded).astype(jnp.bfloat16)
    return tuple((project(normed, weight) for weight in weights))


def per_device(
    byte_values_sequence,
    offsets,
    byte_table,
    byte_query,
    byte_key,
    byte_value,
    latent_query,
    latent_key,
    latent_value,
    decode_weight,
):
    row_count = byte_values_sequence.shape[0]
    channels = byte_query.shape[1]
    heads_here = HEADS_B * channels // DB
    head_feature_width = channels // heads_here
    ctx_count = lax.axis_size("ctx")
    tp_count = lax.axis_size("tp")
    slot_cap = 3 * row_count // 8
    block_index = lax.axis_index(("bytes", "ctx"))
    byte_window_queries, byte_window_keys, values_b = byte_project(
        byte_values_sequence, byte_table, (byte_query, byte_key, byte_value)
    )
    keys_e, values_e = from_behind((byte_window_keys, values_b), ("bytes", "ctx"), 1)
    keys_w = jnp.concatenate([keys_e, byte_window_keys], axis=0).reshape(
        2 * row_count, heads_here, head_feature_width
    )
    values_w = jnp.concatenate([values_e, values_b], axis=0).reshape(
        2 * row_count, heads_here, head_feature_width
    )
    queries_w = byte_window_queries.reshape(row_count, heads_here, head_feature_width)
    query_pos = jnp.arange(row_count, dtype=jnp.int32)[:, None]
    key_pos = jnp.arange(2 * row_count, dtype=jnp.int32)[None, :]
    allowed_b = (
        (key_pos > query_pos)
        & (key_pos <= query_pos + row_count)
        & ((key_pos >= row_count) | (block_index > 0))
    )
    scores_b = jnp.einsum(
        "qhd,khd->hqk", queries_w, keys_w, preferred_element_type=jnp.float32
    ) / math.sqrt(head_feature_width)
    scores_b = jnp.where(allowed_b[None], scores_b, NEGATIVE)
    highest_b = jnp.max(scores_b, axis=-1, keepdims=True)
    weights_b = jnp.where(allowed_b[None], jnp.exp(scores_b - highest_b), 0.0)
    totals_b = jnp.sum(weights_b, axis=-1)
    blended = jnp.einsum(
        "hqk,khd->qhd", weights_b.astype(jnp.bfloat16), values_w, preferred_element_type=jnp.float32
    )
    encoded = (blended / totals_b.T[:, :, None]).reshape(row_count, channels).astype(jnp.bfloat16)
    starts = (offsets == 0).astype(jnp.int32)
    local_patch = jnp.cumsum(starts) - 1
    members = local_patch[None, :] == jnp.arange(slot_cap, dtype=jnp.int32)[:, None]
    patch_sums = jnp.dot(members.astype(jnp.bfloat16), encoded, preferred_element_type=jnp.float32)
    lengths = jnp.sum(members.astype(jnp.float32), axis=1)
    pooled = (patch_sums / jnp.maximum(lengths, 1.0)[:, None]).astype(jnp.bfloat16)
    gathered, patch_counts = (
        lax.all_gather(pooled, ("ctx", "tp"), axis=0, tiled=True),
        lax.all_gather(local_patch[-1:] + 1, ("ctx", "tp"), axis=0, tiled=True),
    )
    features = gathered.reshape(ctx_count, tp_count, slot_cap, channels).transpose(0, 2, 1, 3)
    features = features.reshape(ctx_count * slot_cap, tp_count * channels)
    patch_counts = patch_counts.reshape(ctx_count, tp_count)[:, 0]
    slot_ids = jnp.arange(slot_cap, dtype=jnp.int32)
    block_ids = lax.axis_index("bytes") * ctx_count + jnp.arange(ctx_count, dtype=jnp.int32)
    positions = jnp.where(
        slot_ids[None, :] < patch_counts[:, None],
        block_ids[:, None] * slot_cap + slot_ids[None, :],
        FARAWAY,
    ).reshape(-1)
    capacity = ctx_count * row_count // 4
    running = jnp.cumsum((positions < FARAWAY).astype(jnp.int32))
    targets = jnp.arange(capacity, dtype=jnp.int32)
    chosen = jnp.minimum(jnp.searchsorted(running, targets + 1), running.shape[0] - 1)
    latent_in = norm_rows(features).astype(jnp.bfloat16)
    queries_l = project(latent_in, latent_query)
    keys_l = project(latent_in, latent_key)
    values_l = project(latent_in, latent_value)
    query_rows = queries_l.shape[0]
    heads_latent = queries_l.shape[1] // HEAD_L
    queries_h = queries_l.reshape(query_rows, heads_latent, HEAD_L)
    initial = (
        jnp.full((heads_latent, query_rows), NEGATIVE, jnp.float32),
        jnp.zeros((heads_latent, query_rows), jnp.float32),
        jnp.zeros((query_rows, heads_latent, HEAD_L), jnp.float32),
    )
    running_state = initial
    keys_p = lax.all_gather(keys_l, "bytes", axis=0, tiled=True)
    values_p = lax.all_gather(values_l, "bytes", axis=0, tiled=True)
    places_p = lax.all_gather(positions, "bytes", axis=0, tiled=True)
    span_rows = keys_p.shape[0]

    def attend_block(state, step_index):
        highest, totals, accumulated = state
        keys_s = lax.dynamic_slice_in_dim(keys_p, step_index * query_rows, query_rows, 0).reshape(
            query_rows, heads_latent, HEAD_L
        )
        values_s = lax.dynamic_slice_in_dim(
            values_p, step_index * query_rows, query_rows, 0
        ).reshape(query_rows, heads_latent, HEAD_L)
        places = lax.dynamic_slice_in_dim(places_p, step_index * query_rows, query_rows, 0)
        attention_scores = jnp.einsum(
            "qhd,khd->hqk", queries_h, keys_s, preferred_element_type=jnp.float32
        ) / math.sqrt(HEAD_L)
        allowed = (places[None, :] <= positions[:, None])[None]
        highest_new = jnp.maximum(
            highest, jnp.max(jnp.where(allowed, attention_scores, NEGATIVE), axis=-1)
        )
        factor = jnp.exp(highest - highest_new)
        weights = jnp.where(allowed, jnp.exp(attention_scores - highest_new[:, :, None]), 0.0)
        totals = totals * factor + jnp.sum(weights, axis=-1)
        mixed_in = jnp.einsum(
            "hqk,khd->qhd",
            weights.astype(jnp.bfloat16),
            values_s,
            preferred_element_type=jnp.float32,
        )
        accumulated = accumulated * factor.T[:, :, None] + mixed_in
        return ((highest_new, totals, accumulated), None)

    running_state, _ = lax.scan(
        attend_block, running_state, jnp.arange(span_rows // query_rows, dtype=jnp.int32)
    )
    highest_l, totals_l, accumulated_l = running_state
    latent_out = (
        (accumulated_l / totals_l.T[:, :, None])
        .reshape(query_rows, heads_latent * HEAD_L)
        .astype(jnp.bfloat16)
    )
    compact = latent_out[chosen]
    shares = lax.psum_scatter(
        jnp.dot(compact, decode_weight, preferred_element_type=jnp.float32).astype(jnp.bfloat16),
        ("ctx", "tp"),
        scatter_dimension=0,
        tiled=True,
    ).astype(jnp.float32)
    summed = lax.all_gather(shares.astype(jnp.bfloat16), ("ctx", "tp"), axis=0, tiled=True).astype(
        shares.dtype
    )
    before = jnp.sum(
        jnp.where(jnp.arange(ctx_count, dtype=jnp.int32) < lax.axis_index("ctx"), patch_counts, 0)
    )
    mine = lax.dynamic_slice_in_dim(summed, lax.axis_index("tp") * channels, channels, 1)
    decoded_bytes = mine[before + local_patch]
    return (encoded.astype(jnp.float32) + decoded_bytes).astype(jnp.bfloat16)


def round_up(value, step):
    return -(-value // step) * step


def fused_kernel(
    bytes_count,
    ctx_count,
    tp_count,
    slot_cap,
    bv_ref,
    off_ref,
    table_hbm,
    wq_hbm,
    wk_hbm,
    wv_hbm,
    lq_hbm,
    lk_hbm,
    lv_hbm,
    dw_hbm,
    out_ref,
    table,
    wb,
    wl,
    dw,
    bv_prev,
    encoded,
    members_ref,
    x_all,
    queries,
    keys,
    values,
    valid,
    bias_ref,
    mixed,
    parts,
    landed,
    load_sems,
    bv_sems,
    z_send,
    z_recv,
    plane_send,
    plane_recv,
    sib_send,
    sib_recv,
    part_send,
    part_recv,
):
    f32, bf16 = jnp.float32, jnp.bfloat16
    z, c, t = lax.axis_index("bytes"), lax.axis_index("ctx"), lax.axis_index("tp")
    rows = bv_ref.shape[1]
    vocab, width = table.shape
    channels = wb.shape[2]
    slots = x_all.shape[2]
    group = ctx_count * slots
    pairs_y = tp_count // 2
    y, core = t // 2, lax.rem(t, 2)
    mesh_ids = pl.DeviceIdType.MESH

    loads = [
        pltpu.make_async_copy(source, target, load_sems.at[index])
        for index, (source, target) in enumerate(
            (
                (table_hbm, table),
                (wq_hbm, wb.at[0]),
                (wk_hbm, wb.at[1]),
                (wv_hbm, wb.at[2]),
                (lq_hbm, wl.at[0]),
                (lk_hbm, wl.at[1]),
                (lv_hbm, wl.at[2]),
                (dw_hbm, dw),
            )
        )
    ]
    for load in loads:
        load.start()

    block = z * ctx_count + c
    blocks = bytes_count * ctx_count
    after = lax.rem(block + 1, blocks)
    earlier = lax.rem(block + blocks - 1, blocks)
    next_id = (after // ctx_count, lax.rem(after, ctx_count), t)
    prev_id = (earlier // ctx_count, lax.rem(earlier, ctx_count), t)

    def plane_peer(i, j):
        return (z, lax.rem(c + i, ctx_count), lax.rem(t + j, tp_count))

    greeted = [next_id, prev_id]
    greeted += [(lax.rem(z + d, bytes_count), c, t) for d in range(1, bytes_count)]
    greeted += [
        plane_peer(i, j) for i in range(ctx_count) for j in range(tp_count) if i or j
    ]
    barrier = pltpu.get_barrier_semaphore()
    for device in greeted:
        pl.semaphore_signal(barrier, inc=1, device_id=device, device_id_type=mesh_ids)

    def remote(source, target, send, recv, device):
        return pltpu.make_async_remote_copy(
            src_ref=source,
            dst_ref=target,
            send_sem=send,
            recv_sem=recv,
            device_id=device,
            device_id_type=mesh_ids,
        )

    pl.semaphore_wait(barrier, len(greeted))
    bv_copy = remote(bv_ref, bv_prev, bv_sems.at[0], bv_sems.at[1], next_id)
    bv_copy.start()

    loads[0].wait()
    table_f = table[...].astype(f32)
    inverse = lax.rsqrt(jnp.mean(table_f * table_f, axis=-1, keepdims=True) + EPSILON)
    normed = (table_f * inverse).astype(bf16)
    tabled = []
    for index in range(3):
        loads[1 + index].wait()
        tabled.append(jnp.dot(normed, wb[index], preferred_element_type=f32).astype(bf16))
    table_q, table_k, table_v = tabled

    starts = (off_ref[...] == 0).astype(f32)
    before = lax.broadcasted_iota(jnp.int32, (rows, rows), 0) <= lax.broadcasted_iota(
        jnp.int32, (rows, rows), 1
    )
    running = jnp.dot(
        jnp.broadcast_to(starts, (16, rows)).astype(bf16),
        before.astype(f32).astype(bf16),
        preferred_element_type=f32,
    )[0:1]
    slot_rows = lax.broadcasted_iota(jnp.int32, (slots, rows), 0).astype(f32)
    members_f = jnp.where(slot_rows == running - 1.0, 1.0, 0.0)
    members = members_f.astype(bf16)
    members_ref[...] = members
    lengths = jnp.sum(members_f, axis=1, keepdims=True)
    patch_count = jnp.sum(starts, axis=1, keepdims=True)

    contract_first = (((0,), (0,)), ((), ()))
    contract_last = (((1,), (1,)), ((), ()))

    def one_hot(ref):
        ids = lax.broadcasted_iota(jnp.int32, (vocab, rows), 0)
        return jnp.where(ids == ref[...], 1.0, 0.0).astype(bf16)

    def pick(hot, source):
        return lax.dot_general(hot, source, contract_first, preferred_element_type=f32).astype(bf16)

    here = one_hot(bv_ref)
    q_b = pick(here, table_q)
    k_here, v_here = pick(here, table_k), pick(here, table_v)
    bv_copy.wait()
    past = one_hot(bv_prev)
    k_b = jnp.concatenate([pick(past, table_k), k_here], axis=0)
    v_b = jnp.concatenate([pick(past, table_v), v_here], axis=0)
    query_pos = lax.broadcasted_iota(jnp.int32, (rows, 2 * rows), 0)
    key_pos = lax.broadcasted_iota(jnp.int32, (rows, 2 * rows), 1)
    first_key = jnp.where(block > 0, 0, rows)
    allowed_b = (key_pos > query_pos) & (key_pos <= query_pos + rows) & (key_pos >= first_key)
    bias_b = jnp.where(allowed_b, 0.0, NEGATIVE)
    head_width = DB // HEADS_B
    factor_b = math.log2(math.e) / math.sqrt(head_width)
    per_tile = 128 // head_width
    lane = lax.broadcasted_iota(jnp.int32, (rows, 128), 1)
    for tile in range(channels // 128):
        columns = slice(tile * 128, (tile + 1) * 128)
        q_t, k_t, v_t = q_b[:, columns], k_b[:, columns], v_b[:, columns]
        blended = None
        for head in range(per_tile):
            inside = (lane >= head * head_width) & (lane < (head + 1) * head_width)
            q_h = jnp.where(inside, q_t.astype(f32), 0.0).astype(bf16)
            scores = lax.dot_general(q_h, k_t, contract_last, preferred_element_type=f32) + bias_b
            weights = jnp.exp2((scores - jnp.max(scores, axis=-1, keepdims=True)) * factor_b)
            totals = jnp.sum(weights, axis=-1, keepdims=True)
            mixed_in = jnp.dot(weights.astype(bf16), v_t, preferred_element_type=f32) / totals
            blended = mixed_in if blended is None else jnp.where(inside, mixed_in, blended)
        encoded[:, columns] = blended.astype(bf16)

    sums = jnp.dot(members, encoded[...], preferred_element_type=f32)
    pooled = sums / jnp.maximum(lengths, 1.0)
    slot_ids = lax.broadcasted_iota(jnp.int32, (slots, channels), 0)
    pooled = jnp.where(slot_ids == slot_cap, patch_count, pooled)
    x_all[t, c] = pooled.astype(bf16)

    def piece(tt, d, cc):
        return x_all.at[tt, d * ctx_count + cc]

    def z_copy(d):
        return remote(
            piece(t, 0, c),
            piece(t, d, c),
            z_send.at[d - 1],
            z_recv.at[d - 1],
            (lax.rem(z + d, bytes_count), c, t),
        )

    hops = [(i, j) for i in range(ctx_count) for j in range(pairs_y)]

    def plane_copy(d, n):
        i, j = hops[n]
        device = (z, lax.rem(c + i, ctx_count), lax.rem(y + j, pairs_y) * 2 + core)
        return remote(
            piece(t, d, c), piece(t, d, c), plane_send.at[d, n], plane_recv.at[d, n], device
        )

    def plane_arrival(d, n):
        i, j = hops[n]
        cc = lax.rem(c + ctx_count - i, ctx_count)
        tt = lax.rem(y + pairs_y - j, pairs_y) * 2 + core
        return piece(tt, d, cc), piece(lax.rem(y + pairs_y - j, pairs_y) * 2 + 1 - core, d, cc)

    def plane_wait(d, n):
        own, _ = plane_arrival(d, n)
        remote(own, own, plane_send.at[d, n], plane_recv.at[d, n], (z, c, t)).wait_recv()

    sibling = (z, c, y * 2 + 1 - core)

    def sib_copy(d, n):
        own, _ = plane_arrival(d, n)
        return remote(own, own, sib_send.at[d, n], sib_recv.at[d, n], sibling)

    def sib_wait(d, n):
        _, other = plane_arrival(d, n)
        remote(other, other, sib_send.at[d, n], sib_recv.at[d, n], sibling).wait_recv()

    def share(d):
        for n in range(len(hops) - 1, 0, -1):
            plane_copy(d, n).start()
        sib_copy(d, 0).start()

    def forward(d):
        for n in range(1, len(hops)):
            plane_wait(d, n)
            sib_copy(d, n).start()

    for d in range(1, bytes_count):
        pl.when(z + d < bytes_count)(lambda d=d: z_copy(d).start())
    share(0)
    for d in range(1, bytes_count):

        def pass_on(d=d):
            z_copy(d).wait_recv()
            share(d)

        pl.when(z >= d)(pass_on)

    for load in loads[4:]:
        load.wait()

    def latent_rows(d):
        for n in range(len(hops)):
            sib_wait(d, n)
        span = slice(d * ctx_count, (d + 1) * ctx_count)
        features = jnp.concatenate(
            [x_all[tt, span].reshape(group, channels) for tt in range(tp_count)], axis=1
        ).astype(f32)
        scale = lax.rsqrt(jnp.mean(features * features, axis=-1, keepdims=True) + EPSILON)
        latent_in = (features * scale).astype(bf16)
        place = slice(d * group, (d + 1) * group)
        if d == 0:
            queries[...] = jnp.dot(latent_in, wl[0], preferred_element_type=f32).astype(bf16)
        keys[place, :] = jnp.dot(latent_in, wl[1], preferred_element_type=f32).astype(bf16)
        values[place, :] = jnp.dot(latent_in, wl[2], preferred_element_type=f32).astype(bf16)
        slot = lax.broadcasted_iota(jnp.int32, (slots, 128), 0).astype(f32)
        for cc in range(ctx_count):
            count = x_all[0, d * ctx_count + cc, slot_cap : slot_cap + 1, 0:128].astype(f32)
            first = (d * ctx_count + cc) * slots
            valid[first : first + slots, :] = jnp.where(slot < count, 1.0, 0.0).astype(bf16)

    def no_rows(d):
        place = slice(d * group, (d + 1) * group)
        keys[place, :] = jnp.zeros_like(keys[place, :])
        values[place, :] = jnp.zeros_like(values[place, :])
        valid[place, :] = jnp.zeros_like(valid[place, :])

    forward(0)
    for d in range(bytes_count):
        if d + 1 < bytes_count:
            pl.when(z >= d + 1)(lambda d=d: forward(d + 1))
        if d == 0:
            latent_rows(0)
        else:
            pl.when(z >= d)(lambda d=d: latent_rows(d))
            pl.when(z < d)(lambda d=d: no_rows(d))

    span_rows = keys.shape[0]
    exists = lax.dot_general(
        jnp.ones((group, 128), bf16), valid[...], contract_last, preferred_element_type=f32
    )
    row_id = lax.broadcasted_iota(jnp.int32, (group, span_rows), 0)
    col_id = lax.broadcasted_iota(jnp.int32, (group, span_rows), 1)
    bias_ref[...] = jnp.where(
        (exists > 0.5) & ((col_id <= row_id) | (col_id >= group)), 0.0, NEGATIVE
    )
    factor_l = math.log2(math.e) / math.sqrt(HEAD_L)
    for head in range(queries.shape[1] // HEAD_L):
        columns = slice(head * HEAD_L, (head + 1) * HEAD_L)
        scores = (
            lax.dot_general(
                queries[:, columns], keys[:, columns], contract_last, preferred_element_type=f32
            )
            + bias_ref[...]
        )
        weights = jnp.exp2((scores - jnp.max(scores, axis=-1, keepdims=True)) * factor_l)
        totals = jnp.sum(weights, axis=-1, keepdims=True)
        head_out = (
            jnp.dot(weights.astype(bf16), values[:, columns], preferred_element_type=f32) / totals
        ).astype(bf16)
        for cc in range(ctx_count):
            mixed[cc, :, columns] = head_out[cc * slots : (cc + 1) * slots]

    def partial_of(i, j):
        cc, tt = lax.rem(c + i, ctx_count), lax.rem(t + j, tp_count)
        columns = pl.ds(pl.multiple_of(tt * channels, channels), channels)
        return jnp.dot(mixed[cc], dw[:, columns], preferred_element_type=f32)

    def part_copy(i, j):
        n = i * tp_count + j
        return remote(
            parts.at[n], landed.at[n], part_send.at[n], part_recv.at[n], plane_peer(i, j)
        )

    others = [(i, j) for i in range(ctx_count - 1, -1, -1) for j in range(tp_count) if i or j]
    for i, j in others:
        parts[i * tp_count + j] = partial_of(i, j).astype(bf16)
        part_copy(i, j).start()
    decoded = partial_of(0, 0)
    for i, j in others:
        part_copy(i, j).wait_recv()
        decoded = decoded + landed[i * tp_count + j].astype(f32)
    high = decoded.astype(bf16)
    low = (decoded - high.astype(f32)).astype(bf16)
    spread = lax.dot_general(
        members_ref[...], high, contract_first, preferred_element_type=f32
    ) + lax.dot_general(members_ref[...], low, contract_first, preferred_element_type=f32)
    out_ref[...] = (encoded[...].astype(f32) + spread).astype(bf16)

    for d in range(1, bytes_count):
        pl.when(z + d < bytes_count)(lambda d=d: z_copy(d).wait_send())

    def shared(d):
        for n in range(len(hops)):
            if n:
                plane_copy(d, n).wait_send()
            sib_copy(d, n).wait_send()

    shared(0)
    for d in range(1, bytes_count):
        pl.when(z >= d)(lambda d=d: shared(d))
    for i, j in others:
        part_copy(i, j).wait_send()


def fused_scratch(sizes, rows, vocab, channels, latent_columns):
    bytes_count, ctx_count, tp_count = sizes
    slots = round_up(3 * rows // 8 + 1, 16)
    group = ctx_count * slots
    span = bytes_count * group
    bf16, f32 = jnp.bfloat16, jnp.float32
    return [
        ((vocab, DB), bf16),
        ((3, DB, channels), bf16),
        ((3, DB, latent_columns), bf16),
        ((latent_columns, DB), bf16),
        ((1, rows), jnp.int32),
        ((rows, channels), bf16),
        ((slots, rows), bf16),
        ((tp_count, bytes_count * ctx_count, slots, channels), bf16),
        ((group, latent_columns), bf16),
        ((span, latent_columns), bf16),
        ((span, latent_columns), bf16),
        ((span, 128), bf16),
        ((group, span), f32),
        ((ctx_count, slots, latent_columns), bf16),
        ((ctx_count * tp_count, slots, channels), bf16),
        ((ctx_count * tp_count, slots, channels), bf16),
    ]


VMEM_BYTES = 60000 * 1024


def fused_fits(sizes, rows, vocab, channels, latent_columns):
    shapes = fused_scratch(sizes, rows, vocab, channels, latent_columns)
    held = sum(math.prod(shape) * jnp.dtype(kind).itemsize for shape, kind in shapes)
    score_bytes = 4 * math.prod(shapes[12][0])
    return sizes[2] % 2 == 0 and held + 6 * score_bytes < VMEM_BYTES


def fused_device(sizes, *args):
    (bv, offsets, table, wq, wk, wv, lq, lk, lv, dw) = args
    bytes_count, ctx_count, tp_count = sizes
    rows, channels = bv.shape[0], wq.shape[1]
    shapes = fused_scratch(sizes, rows, table.shape[0], channels, lq.shape[1])
    hops = ctx_count * tp_count // 2
    peers = ctx_count * tp_count
    dma = pltpu.SemaphoreType.DMA
    return pl.pallas_call(
        functools.partial(fused_kernel, *sizes, 3 * rows // 8),
        out_shape=jax.ShapeDtypeStruct((rows, channels), jnp.bfloat16),
        in_specs=[pl.BlockSpec(memory_space=pltpu.VMEM)] * 2
        + [pl.BlockSpec(memory_space=pl.ANY)] * 8,
        out_specs=pl.BlockSpec(memory_space=pltpu.VMEM),
        scratch_shapes=[pltpu.VMEM(shape, kind) for shape, kind in shapes]
        + [
            dma((8,)),
            dma((2,)),
            dma((max(bytes_count - 1, 1),)),
            dma((max(bytes_count - 1, 1),)),
            dma((bytes_count, hops)),
            dma((bytes_count, hops)),
            dma((bytes_count, hops)),
            dma((bytes_count, hops)),
            dma((peers,)),
            dma((peers,)),
        ],
        compiler_params=pltpu.CompilerParams(
            collective_id=0, has_side_effects=True, vmem_limit_bytes=VMEM_BYTES
        ),
        name="fused",
    )(bv.reshape(1, rows), offsets.reshape(1, rows), table, wq, wk, wv, lq, lk, lv, dw)


def dispatch(sizes, *args):
    rows, vocab = args[0].shape[0], args[2].shape[0]
    channels, latent_columns = args[3].shape[1], args[6].shape[1]
    if fused_fits(sizes, rows, vocab, channels, latent_columns):
        return fused_device(sizes, *args)
    return per_device(*args)


def solution(mesh):
    return jax.shard_map(
        functools.partial(dispatch, tuple(mesh.shape[a] for a in ("bytes", "ctx", "tp"))),
        mesh=mesh,
        in_specs=(
            P(("bytes", "ctx")),
            P(("bytes", "ctx")),
            P(),
            P(None, "tp"),
            P(None, "tp"),
            P(None, "tp"),
            P(None, ("ctx", "tp")),
            P(None, ("ctx", "tp")),
            P(None, ("ctx", "tp")),
            P(("ctx", "tp"), None),
        ),
        out_specs=P(("bytes", "ctx"), "tp"),
        check_vma=False,
    )
```

```python
import functools
import math

import jax
import jax.numpy as jnp
from jax import lax
from jax.experimental import pallas as pl
from jax.experimental.pallas import tpu as pltpu
from jax.sharding import PartitionSpec as P

DB = 1024
HEADS_B = 16
HEAD_L = 128


EPSILON = 1e-06
NEGATIVE = -1e30
FARAWAY = 1 << 30


def from_behind(value, axis, steps):
    count = lax.axis_size(axis)
    first, last = (max(0, -steps), min(count, count - steps))
    return lax.ppermute(value, axis, [(source, source + steps) for source in range(first, last)])


def norm_rows(values):
    values = values.astype(jnp.float32)
    return values * lax.rsqrt(jnp.mean(values * values, axis=-1, keepdims=True) + EPSILON)


def project(inputs, weight):
    return jnp.dot(inputs, weight, preferred_element_type=jnp.float32).astype(jnp.bfloat16)


def byte_project(byte_values_sequence, byte_table, weights):
    onehot = (
        byte_values_sequence[:, None] == jnp.arange(byte_table.shape[0], dtype=jnp.int32)[None, :]
    ).astype(jnp.bfloat16)
    embedded = jnp.dot(onehot, byte_table, preferred_element_type=jnp.float32)
    normed = norm_rows(embedded).astype(jnp.bfloat16)
    return tuple((project(normed, weight) for weight in weights))


def per_device(
    byte_values_sequence,
    offsets,
    byte_table,
    byte_query,
    byte_key,
    byte_value,
    latent_query,
    latent_key,
    latent_value,
    decode_weight,
):
    row_count = byte_values_sequence.shape[0]
    channels = byte_query.shape[1]
    heads_here = HEADS_B * channels // DB
    head_feature_width = channels // heads_here
    ctx_count = lax.axis_size("ctx")
    tp_count = lax.axis_size("tp")
    slot_cap = 3 * row_count // 8
    block_index = lax.axis_index(("bytes", "ctx"))
    byte_window_queries, byte_window_keys, values_b = byte_project(
        byte_values_sequence, byte_table, (byte_query, byte_key, byte_value)
    )
    keys_e, values_e = from_behind((byte_window_keys, values_b), ("bytes", "ctx"), 1)
    keys_w = jnp.concatenate([keys_e, byte_window_keys], axis=0).reshape(
        2 * row_count, heads_here, head_feature_width
    )
    values_w = jnp.concatenate([values_e, values_b], axis=0).reshape(
        2 * row_count, heads_here, head_feature_width
    )
    queries_w = byte_window_queries.reshape(row_count, heads_here, head_feature_width)
    query_pos = jnp.arange(row_count, dtype=jnp.int32)[:, None]
    key_pos = jnp.arange(2 * row_count, dtype=jnp.int32)[None, :]
    allowed_b = (
        (key_pos > query_pos)
        & (key_pos <= query_pos + row_count)
        & ((key_pos >= row_count) | (block_index > 0))
    )
    scores_b = jnp.einsum(
        "qhd,khd->hqk", queries_w, keys_w, preferred_element_type=jnp.float32
    ) / math.sqrt(head_feature_width)
    scores_b = jnp.where(allowed_b[None], scores_b, NEGATIVE)
    highest_b = jnp.max(scores_b, axis=-1, keepdims=True)
    weights_b = jnp.where(allowed_b[None], jnp.exp(scores_b - highest_b), 0.0)
    totals_b = jnp.sum(weights_b, axis=-1)
    blended = jnp.einsum(
        "hqk,khd->qhd", weights_b.astype(jnp.bfloat16), values_w, preferred_element_type=jnp.float32
    )
    encoded = (blended / totals_b.T[:, :, None]).reshape(row_count, channels).astype(jnp.bfloat16)
    starts = (offsets == 0).astype(jnp.int32)
    local_patch = jnp.cumsum(starts) - 1
    members = local_patch[None, :] == jnp.arange(slot_cap, dtype=jnp.int32)[:, None]
    patch_sums = jnp.dot(members.astype(jnp.bfloat16), encoded, preferred_element_type=jnp.float32)
    lengths = jnp.sum(members.astype(jnp.float32), axis=1)
    pooled = (patch_sums / jnp.maximum(lengths, 1.0)[:, None]).astype(jnp.bfloat16)
    gathered, patch_counts = (
        lax.all_gather(pooled, ("ctx", "tp"), axis=0, tiled=True),
        lax.all_gather(local_patch[-1:] + 1, ("ctx", "tp"), axis=0, tiled=True),
    )
    features = gathered.reshape(ctx_count, tp_count, slot_cap, channels).transpose(0, 2, 1, 3)
    features = features.reshape(ctx_count * slot_cap, tp_count * channels)
    patch_counts = patch_counts.reshape(ctx_count, tp_count)[:, 0]
    slot_ids = jnp.arange(slot_cap, dtype=jnp.int32)
    block_ids = lax.axis_index("bytes") * ctx_count + jnp.arange(ctx_count, dtype=jnp.int32)
    positions = jnp.where(
        slot_ids[None, :] < patch_counts[:, None],
        block_ids[:, None] * slot_cap + slot_ids[None, :],
        FARAWAY,
    ).reshape(-1)
    capacity = ctx_count * row_count // 4
    running = jnp.cumsum((positions < FARAWAY).astype(jnp.int32))
    targets = jnp.arange(capacity, dtype=jnp.int32)
    chosen = jnp.minimum(jnp.searchsorted(running, targets + 1), running.shape[0] - 1)
    latent_in = norm_rows(features).astype(jnp.bfloat16)
    queries_l = project(latent_in, latent_query)
    keys_l = project(latent_in, latent_key)
    values_l = project(latent_in, latent_value)
    query_rows = queries_l.shape[0]
    heads_latent = queries_l.shape[1] // HEAD_L
    queries_h = queries_l.reshape(query_rows, heads_latent, HEAD_L)
    initial = (
        jnp.full((heads_latent, query_rows), NEGATIVE, jnp.float32),
        jnp.zeros((heads_latent, query_rows), jnp.float32),
        jnp.zeros((query_rows, heads_latent, HEAD_L), jnp.float32),
    )
    running_state = initial
    keys_p = lax.all_gather(keys_l, "bytes", axis=0, tiled=True)
    values_p = lax.all_gather(values_l, "bytes", axis=0, tiled=True)
    places_p = lax.all_gather(positions, "bytes", axis=0, tiled=True)
    span_rows = keys_p.shape[0]

    def attend_block(state, step_index):
        highest, totals, accumulated = state
        keys_s = lax.dynamic_slice_in_dim(keys_p, step_index * query_rows, query_rows, 0).reshape(
            query_rows, heads_latent, HEAD_L
        )
        values_s = lax.dynamic_slice_in_dim(
            values_p, step_index * query_rows, query_rows, 0
        ).reshape(query_rows, heads_latent, HEAD_L)
        places = lax.dynamic_slice_in_dim(places_p, step_index * query_rows, query_rows, 0)
        attention_scores = jnp.einsum(
            "qhd,khd->hqk", queries_h, keys_s, preferred_element_type=jnp.float32
        ) / math.sqrt(HEAD_L)
        allowed = (places[None, :] <= positions[:, None])[None]
        highest_new = jnp.maximum(
            highest, jnp.max(jnp.where(allowed, attention_scores, NEGATIVE), axis=-1)
        )
        factor = jnp.exp(highest - highest_new)
        weights = jnp.where(allowed, jnp.exp(attention_scores - highest_new[:, :, None]), 0.0)
        totals = totals * factor + jnp.sum(weights, axis=-1)
        mixed_in = jnp.einsum(
            "hqk,khd->qhd",
            weights.astype(jnp.bfloat16),
            values_s,
            preferred_element_type=jnp.float32,
        )
        accumulated = accumulated * factor.T[:, :, None] + mixed_in
        return ((highest_new, totals, accumulated), None)

    running_state, _ = lax.scan(
        attend_block, running_state, jnp.arange(span_rows // query_rows, dtype=jnp.int32)
    )
    highest_l, totals_l, accumulated_l = running_state
    latent_out = (
        (accumulated_l / totals_l.T[:, :, None])
        .reshape(query_rows, heads_latent * HEAD_L)
        .astype(jnp.bfloat16)
    )
    compact = latent_out[chosen]
    shares = lax.psum_scatter(
        jnp.dot(compact, decode_weight, preferred_element_type=jnp.float32).astype(jnp.bfloat16),
        ("ctx", "tp"),
        scatter_dimension=0,
        tiled=True,
    ).astype(jnp.float32)
    summed = lax.all_gather(shares.astype(jnp.bfloat16), ("ctx", "tp"), axis=0, tiled=True).astype(
        shares.dtype
    )
    before = jnp.sum(
        jnp.where(jnp.arange(ctx_count, dtype=jnp.int32) < lax.axis_index("ctx"), patch_counts, 0)
    )
    mine = lax.dynamic_slice_in_dim(summed, lax.axis_index("tp") * channels, channels, 1)
    decoded_bytes = mine[before + local_patch]
    return (encoded.astype(jnp.float32) + decoded_bytes).astype(jnp.bfloat16)


def round_up(value, step):
    return -(-value // step) * step


def fused_kernel(
    bytes_count,
    ctx_count,
    tp_count,
    slot_cap,
    bv_ref,
    off_ref,
    table_hbm,
    wq_hbm,
    wk_hbm,
    wv_hbm,
    lq_hbm,
    lk_hbm,
    lv_hbm,
    dw_hbm,
    out_ref,
    table,
    wb,
    wl,
    dw,
    bv_prev,
    encoded,
    members_ref,
    x_all,
    queries,
    keys,
    values,
    valid,
    bias_ref,
    mixed,
    parts,
    landed,
    load_sems,
    bv_sems,
    z_send,
    z_recv,
    plane_send,
    plane_recv,
    sib_send,
    sib_recv,
    part_send,
    part_recv,
):
    f32, bf16 = jnp.float32, jnp.bfloat16
    z, c, t = lax.axis_index("bytes"), lax.axis_index("ctx"), lax.axis_index("tp")
    rows = bv_ref.shape[1]
    vocab, width = table.shape
    channels = wb.shape[2]
    slots = x_all.shape[2]
    group = ctx_count * slots
    pairs_y = tp_count // 2
    y, core = t // 2, lax.rem(t, 2)
    mesh_ids = pl.DeviceIdType.MESH

    loads = [
        pltpu.make_async_copy(source, target, load_sems.at[index])
        for index, (source, target) in enumerate(
            (
                (table_hbm, table),
                (wq_hbm, wb.at[0]),
                (wk_hbm, wb.at[1]),
                (wv_hbm, wb.at[2]),
                (lq_hbm, wl.at[0]),
                (lk_hbm, wl.at[1]),
                (lv_hbm, wl.at[2]),
                (dw_hbm, dw),
            )
        )
    ]
    for load in loads:
        load.start()

    block = z * ctx_count + c
    blocks = bytes_count * ctx_count
    after = lax.rem(block + 1, blocks)
    earlier = lax.rem(block + blocks - 1, blocks)
    next_id = (after // ctx_count, lax.rem(after, ctx_count), t)
    prev_id = (earlier // ctx_count, lax.rem(earlier, ctx_count), t)

    hops = [(i, j) for i in range(ctx_count) for j in range(pairs_y)]

    def hop_id(n):
        i, j = hops[n]
        return (z, lax.rem(c + i, ctx_count), lax.rem(y + j, pairs_y) * 2 + core)

    sibling = (z, c, y * 2 + 1 - core)
    barrier = pltpu.get_barrier_semaphore()

    def greet(device):
        pl.semaphore_signal(barrier, inc=1, device_id=device, device_id_type=mesh_ids)

    for device in [sibling] + [hop_id(n) for n in range(1, len(hops))]:
        greet(device)
    expected = len(hops)
    near = [
        ((z + step >= 0) & (z + step < bytes_count), (z + step, c, t))
        for step in (-2, -1, 1, 2)
        if abs(step) < bytes_count
    ]
    near += [(block > 0, prev_id), (block + 1 < blocks, next_id)]
    for present, device in near:
        pl.when(present)(lambda device=device: greet(device))
        expected = expected + jnp.where(present, 1, 0)

    def remote(source, target, send, recv, device):
        return pltpu.make_async_remote_copy(
            src_ref=source,
            dst_ref=target,
            send_sem=send,
            recv_sem=recv,
            device_id=device,
            device_id_type=mesh_ids,
        )

    pl.semaphore_wait(barrier, expected)
    bv_copy = remote(bv_ref, bv_prev, bv_sems.at[0], bv_sems.at[1], next_id)

    @pl.when(block == 0)
    def _():
        bv_prev[...] = jnp.zeros_like(bv_prev)

    pl.when(block + 1 < blocks)(bv_copy.start)

    loads[0].wait()
    table_f = table[...].astype(f32)
    inverse = lax.rsqrt(jnp.mean(table_f * table_f, axis=-1, keepdims=True) + EPSILON)
    normed = (table_f * inverse).astype(bf16)
    tabled = []
    for index in range(3):
        loads[1 + index].wait()
        tabled.append(jnp.dot(normed, wb[index], preferred_element_type=f32).astype(bf16))
    table_q, table_k, table_v = tabled

    starts = (off_ref[...] == 0).astype(f32)
    before = lax.broadcasted_iota(jnp.int32, (rows, rows), 0) <= lax.broadcasted_iota(
        jnp.int32, (rows, rows), 1
    )
    running = jnp.dot(
        jnp.broadcast_to(starts, (16, rows)).astype(bf16),
        before.astype(f32).astype(bf16),
        preferred_element_type=f32,
    )[0:1]
    slot_rows = lax.broadcasted_iota(jnp.int32, (slots, rows), 0).astype(f32)
    members_f = jnp.where(slot_rows == running - 1.0, 1.0, 0.0)
    members = members_f.astype(bf16)
    members_ref[...] = members
    lengths = jnp.sum(members_f, axis=1, keepdims=True)
    patch_count = jnp.sum(starts, axis=1, keepdims=True)

    contract_first = (((0,), (0,)), ((), ()))
    contract_last = (((1,), (1,)), ((), ()))

    def one_hot(ref):
        ids = lax.broadcasted_iota(jnp.int32, (vocab, rows), 0)
        return jnp.where(ids == ref[...], 1.0, 0.0).astype(bf16)

    def pick(hot, source):
        return lax.dot_general(hot, source, contract_first, preferred_element_type=f32).astype(bf16)

    here = one_hot(bv_ref)
    q_b = pick(here, table_q)
    k_here, v_here = pick(here, table_k), pick(here, table_v)
    pl.when(block > 0)(bv_copy.wait_recv)
    past = one_hot(bv_prev)
    k_b = jnp.concatenate([pick(past, table_k), k_here], axis=0)
    v_b = jnp.concatenate([pick(past, table_v), v_here], axis=0)
    query_pos = lax.broadcasted_iota(jnp.int32, (rows, 2 * rows), 0)
    key_pos = lax.broadcasted_iota(jnp.int32, (rows, 2 * rows), 1)
    first_key = jnp.where(block > 0, 0, rows)
    allowed_b = (key_pos > query_pos) & (key_pos <= query_pos + rows) & (key_pos >= first_key)
    bias_b = jnp.where(allowed_b, 0.0, NEGATIVE)
    head_width = DB // HEADS_B
    factor_b = math.log2(math.e) / math.sqrt(head_width)
    per_tile = 128 // head_width
    lane = lax.broadcasted_iota(jnp.int32, (rows, 128), 1)
    for tile in range(channels // 128):
        columns = slice(tile * 128, (tile + 1) * 128)
        q_t, k_t, v_t = q_b[:, columns], k_b[:, columns], v_b[:, columns]
        blended = None
        for head in range(per_tile):
            inside = (lane >= head * head_width) & (lane < (head + 1) * head_width)
            q_h = jnp.where(inside, q_t.astype(f32), 0.0).astype(bf16)
            scores = lax.dot_general(q_h, k_t, contract_last, preferred_element_type=f32) + bias_b
            weights = jnp.exp2((scores - jnp.max(scores, axis=-1, keepdims=True)) * factor_b)
            totals = jnp.sum(weights, axis=-1, keepdims=True)
            mixed_in = jnp.dot(weights.astype(bf16), v_t, preferred_element_type=f32) / totals
            blended = mixed_in if blended is None else jnp.where(inside, mixed_in, blended)
        encoded[:, columns] = blended.astype(bf16)

    sums = jnp.dot(members, encoded[...], preferred_element_type=f32)
    pooled = sums / jnp.maximum(lengths, 1.0)
    slot_ids = lax.broadcasted_iota(jnp.int32, (slots, channels), 0)
    pooled = jnp.where(slot_ids == slot_cap, patch_count, pooled)
    x_all[t, c] = pooled.astype(bf16)

    def piece(tt, d, cc):
        return x_all.at[tt, d * ctx_count + cc]

    def z_copy(d):
        source, step = (0, d) if d <= 2 else (d - 1, 1)
        return remote(
            piece(t, source, c),
            piece(t, d, c),
            z_send.at[d - 1],
            z_recv.at[d - 1],
            (lax.rem(z + step, bytes_count), c, t),
        )

    def z_sends(d):
        return z + d < bytes_count if d <= 2 else (z >= d - 1) & (z + 1 < bytes_count)

    def plane_copy(d, n):
        own = piece(t, d, c)
        return remote(own, own, plane_send.at[d, n], plane_recv.at[d, n], hop_id(n))

    def plane_arrival(d, n):
        i, j = hops[n]
        cc = lax.rem(c + ctx_count - i, ctx_count)
        tt = lax.rem(y + pairs_y - j, pairs_y) * 2 + core
        return piece(tt, d, cc), piece(lax.rem(y + pairs_y - j, pairs_y) * 2 + 1 - core, d, cc)

    def plane_wait(d, n):
        own, _ = plane_arrival(d, n)
        remote(own, own, plane_send.at[d, n], plane_recv.at[d, n], (z, c, t)).wait_recv()

    def sib_copy(d, n):
        own, _ = plane_arrival(d, n)
        return remote(own, own, sib_send.at[d, n], sib_recv.at[d, n], sibling)

    def sib_wait(d, n):
        _, other = plane_arrival(d, n)
        remote(other, other, sib_send.at[d, n], sib_recv.at[d, n], sibling).wait_recv()

    def share(d):
        for n in range(len(hops) - 1, 0, -1):
            plane_copy(d, n).start()
        sib_copy(d, 0).start()

    def forward(d):
        for n in range(1, len(hops)):
            plane_wait(d, n)
            sib_copy(d, n).start()

    for d in range(1, min(bytes_count, 3)):
        pl.when(z_sends(d))(lambda d=d: z_copy(d).start())
    share(0)
    for d in range(1, bytes_count):

        def pass_on(d=d):
            z_copy(d).wait_recv()
            if d >= 2 and d + 1 < bytes_count:
                pl.when(z_sends(d + 1))(lambda: z_copy(d + 1).start())
            share(d)

        pl.when(z >= d)(pass_on)

    for load in loads[4:]:
        load.wait()

    def latent_rows(d):
        for n in range(len(hops)):
            sib_wait(d, n)
        span = slice(d * ctx_count, (d + 1) * ctx_count)
        features = jnp.concatenate(
            [x_all[tt, span].reshape(group, channels) for tt in range(tp_count)], axis=1
        ).astype(f32)
        scale = lax.rsqrt(jnp.mean(features * features, axis=-1, keepdims=True) + EPSILON)
        latent_in = (features * scale).astype(bf16)
        place = slice(d * group, (d + 1) * group)
        if d == 0:
            queries[...] = jnp.dot(latent_in, wl[0], preferred_element_type=f32).astype(bf16)
        keys[place, :] = jnp.dot(latent_in, wl[1], preferred_element_type=f32).astype(bf16)
        values[place, :] = jnp.dot(latent_in, wl[2], preferred_element_type=f32).astype(bf16)
        slot = lax.broadcasted_iota(jnp.int32, (slots, 128), 0).astype(f32)
        for cc in range(ctx_count):
            count = x_all[0, d * ctx_count + cc, slot_cap : slot_cap + 1, 0:128].astype(f32)
            first = (d * ctx_count + cc) * slots
            valid[first : first + slots, :] = jnp.where(slot < count, 1.0, 0.0).astype(bf16)

    def no_rows(d):
        place = slice(d * group, (d + 1) * group)
        keys[place, :] = jnp.zeros_like(keys[place, :])
        values[place, :] = jnp.zeros_like(values[place, :])
        valid[place, :] = jnp.zeros_like(valid[place, :])

    forward(0)
    for d in range(bytes_count):
        if d + 1 < bytes_count:
            pl.when(z >= d + 1)(lambda d=d: forward(d + 1))
        if d == 0:
            latent_rows(0)
        else:
            pl.when(z >= d)(lambda d=d: latent_rows(d))
            pl.when(z < d)(lambda d=d: no_rows(d))

    span_rows = keys.shape[0]
    exists = lax.dot_general(
        jnp.ones((group, 128), bf16), valid[...], contract_last, preferred_element_type=f32
    )
    row_id = lax.broadcasted_iota(jnp.int32, (group, span_rows), 0)
    col_id = lax.broadcasted_iota(jnp.int32, (group, span_rows), 1)
    bias_ref[...] = jnp.where(
        (exists > 0.5) & ((col_id <= row_id) | (col_id >= group)), 0.0, NEGATIVE
    )
    factor_l = math.log2(math.e) / math.sqrt(HEAD_L)
    for head in range(queries.shape[1] // HEAD_L):
        columns = slice(head * HEAD_L, (head + 1) * HEAD_L)
        scores = (
            lax.dot_general(
                queries[:, columns], keys[:, columns], contract_last, preferred_element_type=f32
            )
            + bias_ref[...]
        )
        weights = jnp.exp2((scores - jnp.max(scores, axis=-1, keepdims=True)) * factor_l)
        totals = jnp.sum(weights, axis=-1, keepdims=True)
        head_out = (
            jnp.dot(weights.astype(bf16), values[:, columns], preferred_element_type=f32) / totals
        ).astype(bf16)
        for cc in range(ctx_count):
            mixed[cc, :, columns] = head_out[cc * slots : (cc + 1) * slots]

    def partial_of(n, parity):
        i, j = hops[n]
        cc, tt = lax.rem(c + i, ctx_count), lax.rem(y + j, pairs_y) * 2 + parity
        columns = pl.ds(pl.multiple_of(tt * channels, channels), channels)
        return jnp.dot(mixed[cc], dw[:, columns], preferred_element_type=f32)

    def part_copy(n, device):
        return remote(parts.at[n], landed.at[n], part_send.at[n], part_recv.at[n], device)

    count = len(hops)
    farthest_first = list(range(count - 1, -1, -1))
    for n in farthest_first:
        parts[n] = partial_of(n, 1 - core).astype(bf16)
        part_copy(n, sibling).start()
    for n in farthest_first:
        decoded = partial_of(n, core)
        part_copy(n, sibling).wait_recv()
        decoded = decoded + landed[n].astype(f32)
        if n:
            parts[count + n] = decoded.astype(bf16)
            part_copy(count + n, hop_id(n)).start()
    for n in farthest_first[:-1]:
        part_copy(count + n, hop_id(n)).wait_recv()
        decoded = decoded + landed[count + n].astype(f32)
    high = decoded.astype(bf16)
    low = (decoded - high.astype(f32)).astype(bf16)
    spread = lax.dot_general(
        members_ref[...], high, contract_first, preferred_element_type=f32
    ) + lax.dot_general(members_ref[...], low, contract_first, preferred_element_type=f32)
    out_ref[...] = encoded[...].astype(f32) + spread

    pl.when(block + 1 < blocks)(bv_copy.wait_send)
    for d in range(1, bytes_count):
        pl.when(z_sends(d))(lambda d=d: z_copy(d).wait_send())

    def shared(d):
        for n in range(len(hops)):
            if n:
                plane_copy(d, n).wait_send()
            sib_copy(d, n).wait_send()

    shared(0)
    for d in range(1, bytes_count):
        pl.when(z >= d)(lambda d=d: shared(d))
    for n in farthest_first:
        part_copy(n, sibling).wait_send()
        if n:
            part_copy(count + n, hop_id(n)).wait_send()


def fused_scratch(sizes, rows, vocab, channels, latent_columns):
    bytes_count, ctx_count, tp_count = sizes
    slots = round_up(3 * rows // 8 + 1, 16)
    group = ctx_count * slots
    span = bytes_count * group
    bf16, f32 = jnp.bfloat16, jnp.float32
    return [
        ((vocab, DB), bf16),
        ((3, DB, channels), bf16),
        ((3, DB, latent_columns), bf16),
        ((latent_columns, DB), bf16),
        ((1, rows), jnp.int32),
        ((rows, channels), bf16),
        ((slots, rows), bf16),
        ((tp_count, bytes_count * ctx_count, slots, channels), bf16),
        ((group, latent_columns), bf16),
        ((span, latent_columns), bf16),
        ((span, latent_columns), bf16),
        ((span, 128), bf16),
        ((group, span), f32),
        ((ctx_count, slots, latent_columns), bf16),
        ((ctx_count * tp_count, slots, channels), bf16),
        ((ctx_count * tp_count, slots, channels), bf16),
    ]


VMEM_BYTES = 60000 * 1024


def fused_fits(sizes, rows, vocab, channels, latent_columns):
    shapes = fused_scratch(sizes, rows, vocab, channels, latent_columns)
    held = sum(math.prod(shape) * jnp.dtype(kind).itemsize for shape, kind in shapes)
    score_bytes = 4 * math.prod(shapes[12][0])
    return sizes[2] % 2 == 0 and held + 6 * score_bytes < VMEM_BYTES


def fused_device(sizes, *args):
    (bv, offsets, table, wq, wk, wv, lq, lk, lv, dw) = args
    bytes_count, ctx_count, tp_count = sizes
    rows, channels = bv.shape[0], wq.shape[1]
    shapes = fused_scratch(sizes, rows, table.shape[0], channels, lq.shape[1])
    hops = ctx_count * tp_count // 2
    peers = ctx_count * tp_count
    dma = pltpu.SemaphoreType.DMA
    return pl.pallas_call(
        functools.partial(fused_kernel, *sizes, 3 * rows // 8),
        out_shape=jax.ShapeDtypeStruct((rows, channels), jnp.float32),
        in_specs=[pl.BlockSpec(memory_space=pltpu.VMEM)] * 2
        + [pl.BlockSpec(memory_space=pl.ANY)] * 8,
        out_specs=pl.BlockSpec(memory_space=pltpu.VMEM),
        scratch_shapes=[pltpu.VMEM(shape, kind) for shape, kind in shapes]
        + [
            dma((8,)),
            dma((2,)),
            dma((max(bytes_count - 1, 1),)),
            dma((max(bytes_count - 1, 1),)),
            dma((bytes_count, hops)),
            dma((bytes_count, hops)),
            dma((bytes_count, hops)),
            dma((bytes_count, hops)),
            dma((peers,)),
            dma((peers,)),
        ],
        compiler_params=pltpu.CompilerParams(
            collective_id=0, has_side_effects=True, vmem_limit_bytes=VMEM_BYTES
        ),
        name="fused",
    )(bv.reshape(1, rows), offsets.reshape(1, rows), table, wq, wk, wv, lq, lk, lv, dw).astype(jnp.bfloat16)


def dispatch(sizes, *args):
    rows, vocab = args[0].shape[0], args[2].shape[0]
    channels, latent_columns = args[3].shape[1], args[6].shape[1]
    if fused_fits(sizes, rows, vocab, channels, latent_columns):
        return fused_device(sizes, *args)
    return per_device(*args)


def solution(mesh):
    return jax.shard_map(
        functools.partial(dispatch, tuple(mesh.shape[a] for a in ("bytes", "ctx", "tp"))),
        mesh=mesh,
        in_specs=(
            P(("bytes", "ctx")),
            P(("bytes", "ctx")),
            P(),
            P(None, "tp"),
            P(None, "tp"),
            P(None, "tp"),
            P(None, ("ctx", "tp")),
            P(None, ("ctx", "tp")),
            P(None, ("ctx", "tp")),
            P(("ctx", "tp"), None),
        ),
        out_specs=P(("bytes", "ctx"), "tp"),
        check_vma=False,
    )
```

```python
import functools
import math

import jax
import jax.numpy as jnp
from jax import lax
from jax.experimental import pallas as pl
from jax.experimental.pallas import tpu as pltpu
from jax.sharding import PartitionSpec as P

DB = 1024
HEADS_B = 16
HEAD_L = 128


EPSILON = 1e-06
NEGATIVE = -1e30
FARAWAY = 1 << 30


def from_behind(value, axis, steps):
    count = lax.axis_size(axis)
    first, last = (max(0, -steps), min(count, count - steps))
    return lax.ppermute(value, axis, [(source, source + steps) for source in range(first, last)])


def norm_rows(values):
    values = values.astype(jnp.float32)
    return values * lax.rsqrt(jnp.mean(values * values, axis=-1, keepdims=True) + EPSILON)


def project(inputs, weight):
    return jnp.dot(inputs, weight, preferred_element_type=jnp.float32).astype(jnp.bfloat16)


def byte_project(byte_values_sequence, byte_table, weights):
    onehot = (
        byte_values_sequence[:, None] == jnp.arange(byte_table.shape[0], dtype=jnp.int32)[None, :]
    ).astype(jnp.bfloat16)
    embedded = jnp.dot(onehot, byte_table, preferred_element_type=jnp.float32)
    normed = norm_rows(embedded).astype(jnp.bfloat16)
    return tuple((project(normed, weight) for weight in weights))


def per_device(
    byte_values_sequence,
    offsets,
    byte_table,
    byte_query,
    byte_key,
    byte_value,
    latent_query,
    latent_key,
    latent_value,
    decode_weight,
):
    row_count = byte_values_sequence.shape[0]
    channels = byte_query.shape[1]
    heads_here = HEADS_B * channels // DB
    head_feature_width = channels // heads_here
    ctx_count = lax.axis_size("ctx")
    tp_count = lax.axis_size("tp")
    slot_cap = 3 * row_count // 8
    block_index = lax.axis_index(("bytes", "ctx"))
    byte_window_queries, byte_window_keys, values_b = byte_project(
        byte_values_sequence, byte_table, (byte_query, byte_key, byte_value)
    )
    keys_e, values_e = from_behind((byte_window_keys, values_b), ("bytes", "ctx"), 1)
    keys_w = jnp.concatenate([keys_e, byte_window_keys], axis=0).reshape(
        2 * row_count, heads_here, head_feature_width
    )
    values_w = jnp.concatenate([values_e, values_b], axis=0).reshape(
        2 * row_count, heads_here, head_feature_width
    )
    queries_w = byte_window_queries.reshape(row_count, heads_here, head_feature_width)
    query_pos = jnp.arange(row_count, dtype=jnp.int32)[:, None]
    key_pos = jnp.arange(2 * row_count, dtype=jnp.int32)[None, :]
    allowed_b = (
        (key_pos > query_pos)
        & (key_pos <= query_pos + row_count)
        & ((key_pos >= row_count) | (block_index > 0))
    )
    scores_b = jnp.einsum(
        "qhd,khd->hqk", queries_w, keys_w, preferred_element_type=jnp.float32
    ) / math.sqrt(head_feature_width)
    scores_b = jnp.where(allowed_b[None], scores_b, NEGATIVE)
    highest_b = jnp.max(scores_b, axis=-1, keepdims=True)
    weights_b = jnp.where(allowed_b[None], jnp.exp(scores_b - highest_b), 0.0)
    totals_b = jnp.sum(weights_b, axis=-1)
    blended = jnp.einsum(
        "hqk,khd->qhd", weights_b.astype(jnp.bfloat16), values_w, preferred_element_type=jnp.float32
    )
    encoded = (blended / totals_b.T[:, :, None]).reshape(row_count, channels).astype(jnp.bfloat16)
    starts = (offsets == 0).astype(jnp.int32)
    local_patch = jnp.cumsum(starts) - 1
    members = local_patch[None, :] == jnp.arange(slot_cap, dtype=jnp.int32)[:, None]
    patch_sums = jnp.dot(members.astype(jnp.bfloat16), encoded, preferred_element_type=jnp.float32)
    lengths = jnp.sum(members.astype(jnp.float32), axis=1)
    pooled = (patch_sums / jnp.maximum(lengths, 1.0)[:, None]).astype(jnp.bfloat16)
    gathered, patch_counts = (
        lax.all_gather(pooled, ("ctx", "tp"), axis=0, tiled=True),
        lax.all_gather(local_patch[-1:] + 1, ("ctx", "tp"), axis=0, tiled=True),
    )
    features = gathered.reshape(ctx_count, tp_count, slot_cap, channels).transpose(0, 2, 1, 3)
    features = features.reshape(ctx_count * slot_cap, tp_count * channels)
    patch_counts = patch_counts.reshape(ctx_count, tp_count)[:, 0]
    slot_ids = jnp.arange(slot_cap, dtype=jnp.int32)
    block_ids = lax.axis_index("bytes") * ctx_count + jnp.arange(ctx_count, dtype=jnp.int32)
    positions = jnp.where(
        slot_ids[None, :] < patch_counts[:, None],
        block_ids[:, None] * slot_cap + slot_ids[None, :],
        FARAWAY,
    ).reshape(-1)
    capacity = ctx_count * row_count // 4
    running = jnp.cumsum((positions < FARAWAY).astype(jnp.int32))
    targets = jnp.arange(capacity, dtype=jnp.int32)
    chosen = jnp.minimum(jnp.searchsorted(running, targets + 1), running.shape[0] - 1)
    latent_in = norm_rows(features).astype(jnp.bfloat16)
    queries_l = project(latent_in, latent_query)
    keys_l = project(latent_in, latent_key)
    values_l = project(latent_in, latent_value)
    query_rows = queries_l.shape[0]
    heads_latent = queries_l.shape[1] // HEAD_L
    queries_h = queries_l.reshape(query_rows, heads_latent, HEAD_L)
    initial = (
        jnp.full((heads_latent, query_rows), NEGATIVE, jnp.float32),
        jnp.zeros((heads_latent, query_rows), jnp.float32),
        jnp.zeros((query_rows, heads_latent, HEAD_L), jnp.float32),
    )
    running_state = initial
    keys_p = lax.all_gather(keys_l, "bytes", axis=0, tiled=True)
    values_p = lax.all_gather(values_l, "bytes", axis=0, tiled=True)
    places_p = lax.all_gather(positions, "bytes", axis=0, tiled=True)
    span_rows = keys_p.shape[0]

    def attend_block(state, step_index):
        highest, totals, accumulated = state
        keys_s = lax.dynamic_slice_in_dim(keys_p, step_index * query_rows, query_rows, 0).reshape(
            query_rows, heads_latent, HEAD_L
        )
        values_s = lax.dynamic_slice_in_dim(
            values_p, step_index * query_rows, query_rows, 0
        ).reshape(query_rows, heads_latent, HEAD_L)
        places = lax.dynamic_slice_in_dim(places_p, step_index * query_rows, query_rows, 0)
        attention_scores = jnp.einsum(
            "qhd,khd->hqk", queries_h, keys_s, preferred_element_type=jnp.float32
        ) / math.sqrt(HEAD_L)
        allowed = (places[None, :] <= positions[:, None])[None]
        highest_new = jnp.maximum(
            highest, jnp.max(jnp.where(allowed, attention_scores, NEGATIVE), axis=-1)
        )
        factor = jnp.exp(highest - highest_new)
        weights = jnp.where(allowed, jnp.exp(attention_scores - highest_new[:, :, None]), 0.0)
        totals = totals * factor + jnp.sum(weights, axis=-1)
        mixed_in = jnp.einsum(
            "hqk,khd->qhd",
            weights.astype(jnp.bfloat16),
            values_s,
            preferred_element_type=jnp.float32,
        )
        accumulated = accumulated * factor.T[:, :, None] + mixed_in
        return ((highest_new, totals, accumulated), None)

    running_state, _ = lax.scan(
        attend_block, running_state, jnp.arange(span_rows // query_rows, dtype=jnp.int32)
    )
    highest_l, totals_l, accumulated_l = running_state
    latent_out = (
        (accumulated_l / totals_l.T[:, :, None])
        .reshape(query_rows, heads_latent * HEAD_L)
        .astype(jnp.bfloat16)
    )
    compact = latent_out[chosen]
    shares = lax.psum_scatter(
        jnp.dot(compact, decode_weight, preferred_element_type=jnp.float32).astype(jnp.bfloat16),
        ("ctx", "tp"),
        scatter_dimension=0,
        tiled=True,
    ).astype(jnp.float32)
    summed = lax.all_gather(shares.astype(jnp.bfloat16), ("ctx", "tp"), axis=0, tiled=True).astype(
        shares.dtype
    )
    before = jnp.sum(
        jnp.where(jnp.arange(ctx_count, dtype=jnp.int32) < lax.axis_index("ctx"), patch_counts, 0)
    )
    mine = lax.dynamic_slice_in_dim(summed, lax.axis_index("tp") * channels, channels, 1)
    decoded_bytes = mine[before + local_patch]
    return (encoded.astype(jnp.float32) + decoded_bytes).astype(jnp.bfloat16)


def round_up(value, step):
    return -(-value // step) * step


def fused_kernel(
    bytes_count,
    ctx_count,
    tp_count,
    slot_cap,
    bv_ref,
    off_ref,
    table_hbm,
    wq_hbm,
    wk_hbm,
    wv_hbm,
    lq_hbm,
    lk_hbm,
    lv_hbm,
    dw_hbm,
    out_ref,
    table,
    wb,
    wl,
    dw,
    bv_prev,
    encoded,
    members_ref,
    x_all,
    queries,
    keys,
    values,
    valid,
    bias_ref,
    mixed,
    parts,
    landed,
    load_sems,
    bv_sems,
    z_send,
    z_recv,
    plane_send,
    plane_recv,
    sib_send,
    sib_recv,
    part_send,
    part_recv,
):
    f32, bf16 = jnp.float32, jnp.bfloat16
    z, c, t = lax.axis_index("bytes"), lax.axis_index("ctx"), lax.axis_index("tp")
    rows = bv_ref.shape[1]
    vocab, width = table.shape
    channels = wb.shape[2]
    slots = x_all.shape[2]
    group = ctx_count * slots
    pairs_y = tp_count // 2
    y, core = t // 2, lax.rem(t, 2)
    mesh_ids = pl.DeviceIdType.MESH

    loads = [
        pltpu.make_async_copy(source, target, load_sems.at[index])
        for index, (source, target) in enumerate(
            (
                (table_hbm, table),
                (wq_hbm, wb.at[0]),
                (wk_hbm, wb.at[1]),
                (wv_hbm, wb.at[2]),
                (lq_hbm, wl.at[0]),
                (lk_hbm, wl.at[1]),
                (lv_hbm, wl.at[2]),
                (dw_hbm, dw),
            )
        )
    ]
    for load in loads:
        load.start()

    block = z * ctx_count + c
    blocks = bytes_count * ctx_count
    after = lax.rem(block + 1, blocks)
    earlier = lax.rem(block + blocks - 1, blocks)
    next_id = (after // ctx_count, lax.rem(after, ctx_count), t)
    prev_id = (earlier // ctx_count, lax.rem(earlier, ctx_count), t)

    hops = [(i, j) for i in range(ctx_count) for j in range(pairs_y)]

    def hop_id(n):
        i, j = hops[n]
        return (z, lax.rem(c + i, ctx_count), lax.rem(y + j, pairs_y) * 2 + core)

    sibling = (z, c, y * 2 + 1 - core)
    barrier = pltpu.get_barrier_semaphore()

    def greet(device):
        pl.semaphore_signal(barrier, inc=1, device_id=device, device_id_type=mesh_ids)

    for device in [sibling] + [hop_id(n) for n in range(1, len(hops))]:
        greet(device)
    expected = len(hops)
    near = [
        ((z + step >= 0) & (z + step < bytes_count), (z + step, c, t))
        for step in (-2, -1, 1, 2)
        if abs(step) < bytes_count
    ]
    near += [(block > 0, prev_id), (block + 1 < blocks, next_id)]
    for present, device in near:
        pl.when(present)(lambda device=device: greet(device))
        expected = expected + jnp.where(present, 1, 0)

    def remote(source, target, send, recv, device):
        return pltpu.make_async_remote_copy(
            src_ref=source,
            dst_ref=target,
            send_sem=send,
            recv_sem=recv,
            device_id=device,
            device_id_type=mesh_ids,
        )

    pl.semaphore_wait(barrier, expected)
    bv_copy = remote(bv_ref, bv_prev, bv_sems.at[0], bv_sems.at[1], next_id)

    @pl.when(block == 0)
    def _():
        bv_prev[...] = jnp.zeros_like(bv_prev)

    pl.when(block + 1 < blocks)(bv_copy.start)

    loads[0].wait()
    table_f = table[...].astype(f32)
    inverse = lax.rsqrt(jnp.mean(table_f * table_f, axis=-1, keepdims=True) + EPSILON)
    normed = (table_f * inverse).astype(bf16)
    tabled = []
    for index in range(3):
        loads[1 + index].wait()
        tabled.append(jnp.dot(normed, wb[index], preferred_element_type=f32).astype(bf16))
    table_q, table_k, table_v = tabled

    starts = (off_ref[...] == 0).astype(f32)
    before = lax.broadcasted_iota(jnp.int32, (rows, rows), 0) <= lax.broadcasted_iota(
        jnp.int32, (rows, rows), 1
    )
    running = jnp.dot(
        jnp.broadcast_to(starts, (16, rows)).astype(bf16),
        before.astype(f32).astype(bf16),
        preferred_element_type=f32,
    )[0:1]
    slot_rows = lax.broadcasted_iota(jnp.int32, (slots, rows), 0).astype(f32)
    members_f = jnp.where(slot_rows == running - 1.0, 1.0, 0.0)
    members = members_f.astype(bf16)
    members_ref[...] = members
    lengths = jnp.sum(members_f, axis=1, keepdims=True)
    patch_count = jnp.sum(starts, axis=1, keepdims=True)

    contract_first = (((0,), (0,)), ((), ()))
    contract_last = (((1,), (1,)), ((), ()))

    def one_hot(ref):
        ids = lax.broadcasted_iota(jnp.int32, (vocab, rows), 0)
        return jnp.where(ids == ref[...], 1.0, 0.0).astype(bf16)

    def pick(hot, source):
        return lax.dot_general(hot, source, contract_first, preferred_element_type=f32).astype(bf16)

    here = one_hot(bv_ref)
    q_b = pick(here, table_q)
    k_here, v_here = pick(here, table_k), pick(here, table_v)
    pl.when(block > 0)(bv_copy.wait_recv)
    past = one_hot(bv_prev)
    k_b = jnp.concatenate([pick(past, table_k), k_here], axis=0)
    v_b = jnp.concatenate([pick(past, table_v), v_here], axis=0)
    query_pos = lax.broadcasted_iota(jnp.int32, (rows, 2 * rows), 0)
    key_pos = lax.broadcasted_iota(jnp.int32, (rows, 2 * rows), 1)
    first_key = jnp.where(block > 0, 0, rows)
    allowed_b = (key_pos > query_pos) & (key_pos <= query_pos + rows) & (key_pos >= first_key)
    bias_b = jnp.where(allowed_b, 0.0, NEGATIVE)
    head_width = DB // HEADS_B
    factor_b = math.log2(math.e) / math.sqrt(head_width)
    per_tile = 128 // head_width
    lane = lax.broadcasted_iota(jnp.int32, (rows, 128), 1)
    for tile in range(channels // 128):
        columns = slice(tile * 128, (tile + 1) * 128)
        q_t, k_t, v_t = q_b[:, columns], k_b[:, columns], v_b[:, columns]
        blended = None
        for head in range(per_tile):
            inside = (lane >= head * head_width) & (lane < (head + 1) * head_width)
            q_h = jnp.where(inside, q_t.astype(f32), 0.0).astype(bf16)
            scores = lax.dot_general(q_h, k_t, contract_last, preferred_element_type=f32) + bias_b
            weights = jnp.exp2((scores - jnp.max(scores, axis=-1, keepdims=True)) * factor_b)
            totals = jnp.sum(weights, axis=-1, keepdims=True)
            mixed_in = jnp.dot(weights.astype(bf16), v_t, preferred_element_type=f32) / totals
            blended = mixed_in if blended is None else jnp.where(inside, mixed_in, blended)
        encoded[:, columns] = blended.astype(bf16)

    sums = jnp.dot(members, encoded[...], preferred_element_type=f32)
    pooled = sums / jnp.maximum(lengths, 1.0)
    slot_ids = lax.broadcasted_iota(jnp.int32, (slots, channels), 0)
    pooled = jnp.where(slot_ids == slot_cap, patch_count, pooled)
    x_all[t, c] = pooled.astype(bf16)

    def piece(tt, d, cc):
        return x_all.at[tt, d * ctx_count + cc]

    def z_copy(d):
        source, step = (0, d) if d <= 2 else (d - 1, 1)
        return remote(
            piece(t, source, c),
            piece(t, d, c),
            z_send.at[d - 1],
            z_recv.at[d - 1],
            (lax.rem(z + step, bytes_count), c, t),
        )

    def z_sends(d):
        return z + d < bytes_count if d <= 2 else (z >= d - 1) & (z + 1 < bytes_count)

    def plane_copy(d, n):
        own = piece(t, d, c)
        return remote(own, own, plane_send.at[d, n], plane_recv.at[d, n], hop_id(n))

    def plane_arrival(d, n):
        i, j = hops[n]
        cc = lax.rem(c + ctx_count - i, ctx_count)
        tt = lax.rem(y + pairs_y - j, pairs_y) * 2 + core
        return piece(tt, d, cc), piece(lax.rem(y + pairs_y - j, pairs_y) * 2 + 1 - core, d, cc)

    def plane_wait(d, n):
        own, _ = plane_arrival(d, n)
        remote(own, own, plane_send.at[d, n], plane_recv.at[d, n], (z, c, t)).wait_recv()

    def sib_copy(d, n):
        own, _ = plane_arrival(d, n)
        return remote(own, own, sib_send.at[d, n], sib_recv.at[d, n], sibling)

    def sib_wait(d, n):
        _, other = plane_arrival(d, n)
        remote(other, other, sib_send.at[d, n], sib_recv.at[d, n], sibling).wait_recv()

    direct = [n for n, (i, j) in enumerate(hops) if (i == 0) != (j == 0)]
    diagonal = [n for n, (i, j) in enumerate(hops) if i and j]

    def relay_copy(d, n):
        i, j = hops[n]
        even = core == 0
        cc = lax.rem(c + jnp.where(even, ctx_count - i, 0), ctx_count)
        yy = lax.rem(y + jnp.where(even, 0, pairs_y - j), pairs_y)
        to_c = lax.rem(c + jnp.where(even, 0, i), ctx_count)
        to_y = lax.rem(y + jnp.where(even, j, 0), pairs_y)
        passed = piece(yy * 2 + core, d, cc)
        device = (z, to_c, to_y * 2 + core)
        return remote(passed, passed, plane_send.at[d, n], plane_recv.at[d, n], device)

    def share(d):
        for n in direct:
            plane_copy(d, n).start()
        sib_copy(d, 0).start()

    def forward_direct(d):
        for n in direct:
            plane_wait(d, n)
        for n in diagonal:
            relay_copy(d, n).start()
        for n in direct:
            sib_copy(d, n).start()

    def forward_diagonal(d):
        for n in diagonal:
            plane_wait(d, n)
            sib_copy(d, n).start()

    for d in range(1, min(bytes_count, 3)):
        pl.when(z_sends(d))(lambda d=d: z_copy(d).start())
    share(0)

    def take(d):
        z_copy(d).wait_recv()
        if d >= 2 and d + 1 < bytes_count:
            pl.when(z_sends(d + 1))(lambda: z_copy(d + 1).start())
        share(d)

    def latent_rows(d):
        for n in range(len(hops)):
            sib_wait(d, n)
        span = slice(d * ctx_count, (d + 1) * ctx_count)
        features = jnp.concatenate(
            [x_all[tt, span].reshape(group, channels) for tt in range(tp_count)], axis=1
        ).astype(f32)
        scale = lax.rsqrt(jnp.mean(features * features, axis=-1, keepdims=True) + EPSILON)
        latent_in = (features * scale).astype(bf16)
        place = slice(d * group, (d + 1) * group)
        if d == 0:
            queries[...] = jnp.dot(latent_in, wl[0], preferred_element_type=f32).astype(bf16)
        keys[place, :] = jnp.dot(latent_in, wl[1], preferred_element_type=f32).astype(bf16)
        values[place, :] = jnp.dot(latent_in, wl[2], preferred_element_type=f32).astype(bf16)
        slot = lax.broadcasted_iota(jnp.int32, (slots, 128), 0).astype(f32)
        for cc in range(ctx_count):
            count = x_all[0, d * ctx_count + cc, slot_cap : slot_cap + 1, 0:128].astype(f32)
            first = (d * ctx_count + cc) * slots
            valid[first : first + slots, :] = jnp.where(slot < count, 1.0, 0.0).astype(bf16)

    def no_rows(d):
        place = slice(d * group, (d + 1) * group)
        keys[place, :] = jnp.zeros_like(keys[place, :])
        values[place, :] = jnp.zeros_like(values[place, :])
        valid[place, :] = jnp.zeros_like(valid[place, :])

    def when_present(d, action):
        if d == 0:
            action(d)
        elif 0 < d < bytes_count:
            pl.when(z >= d)(lambda: action(d))

    for step in range(1, bytes_count + 3):
        when_present(step, take)
        when_present(step - 1, forward_direct)
        when_present(step - 2, forward_diagonal)
        if step == 3:
            for load in loads[4:]:
                load.wait()
        when_present(step - 3, latent_rows)
        if 0 < step - 3 < bytes_count:
            pl.when(z < step - 3)(lambda d=step - 3: no_rows(d))

    span_rows = keys.shape[0]
    exists = lax.dot_general(
        jnp.ones((group, 128), bf16), valid[...], contract_last, preferred_element_type=f32
    )
    row_id = lax.broadcasted_iota(jnp.int32, (group, span_rows), 0)
    col_id = lax.broadcasted_iota(jnp.int32, (group, span_rows), 1)
    bias_ref[...] = jnp.where(
        (exists > 0.5) & ((col_id <= row_id) | (col_id >= group)), 0.0, NEGATIVE
    )
    factor_l = math.log2(math.e) / math.sqrt(HEAD_L)
    for head in range(queries.shape[1] // HEAD_L):
        columns = slice(head * HEAD_L, (head + 1) * HEAD_L)
        scores = (
            lax.dot_general(
                queries[:, columns], keys[:, columns], contract_last, preferred_element_type=f32
            )
            + bias_ref[...]
        )
        weights = jnp.exp2((scores - jnp.max(scores, axis=-1, keepdims=True)) * factor_l)
        totals = jnp.sum(weights, axis=-1, keepdims=True)
        head_out = (
            jnp.dot(weights.astype(bf16), values[:, columns], preferred_element_type=f32) / totals
        ).astype(bf16)
        for cc in range(ctx_count):
            mixed[cc, :, columns] = head_out[cc * slots : (cc + 1) * slots]

    def partial_of(n, parity):
        i, j = hops[n]
        cc, tt = lax.rem(c + i, ctx_count), lax.rem(y + j, pairs_y) * 2 + parity
        columns = pl.ds(pl.multiple_of(tt * channels, channels), channels)
        return jnp.dot(mixed[cc], dw[:, columns], preferred_element_type=f32)

    def part_copy(n, device):
        return remote(parts.at[n], landed.at[n], part_send.at[n], part_recv.at[n], device)

    count = len(hops)
    farthest_first = list(range(count - 1, -1, -1))
    for n in farthest_first:
        parts[n] = partial_of(n, 1 - core).astype(bf16)
        part_copy(n, sibling).start()
    for n in farthest_first:
        decoded = partial_of(n, core)
        part_copy(n, sibling).wait_recv()
        decoded = decoded + landed[n].astype(f32)
        if n:
            parts[count + n] = decoded.astype(bf16)
            part_copy(count + n, hop_id(n)).start()
    for n in farthest_first[:-1]:
        part_copy(count + n, hop_id(n)).wait_recv()
        decoded = decoded + landed[count + n].astype(f32)
    high = decoded.astype(bf16)
    low = (decoded - high.astype(f32)).astype(bf16)
    spread = lax.dot_general(
        members_ref[...], high, contract_first, preferred_element_type=f32
    ) + lax.dot_general(members_ref[...], low, contract_first, preferred_element_type=f32)
    out_ref[...] = encoded[...].astype(f32) + spread

    pl.when(block + 1 < blocks)(bv_copy.wait_send)
    for d in range(1, bytes_count):
        pl.when(z_sends(d))(lambda d=d: z_copy(d).wait_send())

    def shared(d):
        for n in range(len(hops)):
            if n in direct:
                plane_copy(d, n).wait_send()
            elif n:
                relay_copy(d, n).wait_send()
            sib_copy(d, n).wait_send()

    shared(0)
    for d in range(1, bytes_count):
        pl.when(z >= d)(lambda d=d: shared(d))
    for n in farthest_first:
        part_copy(n, sibling).wait_send()
        if n:
            part_copy(count + n, hop_id(n)).wait_send()


def fused_scratch(sizes, rows, vocab, channels, latent_columns):
    bytes_count, ctx_count, tp_count = sizes
    slots = round_up(3 * rows // 8 + 1, 16)
    group = ctx_count * slots
    span = bytes_count * group
    bf16, f32 = jnp.bfloat16, jnp.float32
    return [
        ((vocab, DB), bf16),
        ((3, DB, channels), bf16),
        ((3, DB, latent_columns), bf16),
        ((latent_columns, DB), bf16),
        ((1, rows), jnp.int32),
        ((rows, channels), bf16),
        ((slots, rows), bf16),
        ((tp_count, bytes_count * ctx_count, slots, channels), bf16),
        ((group, latent_columns), bf16),
        ((span, latent_columns), bf16),
        ((span, latent_columns), bf16),
        ((span, 128), bf16),
        ((group, span), f32),
        ((ctx_count, slots, latent_columns), bf16),
        ((ctx_count * tp_count, slots, channels), bf16),
        ((ctx_count * tp_count, slots, channels), bf16),
    ]


VMEM_BYTES = 60000 * 1024


def fused_fits(sizes, rows, vocab, channels, latent_columns):
    shapes = fused_scratch(sizes, rows, vocab, channels, latent_columns)
    held = sum(math.prod(shape) * jnp.dtype(kind).itemsize for shape, kind in shapes)
    score_bytes = 4 * math.prod(shapes[12][0])
    return sizes[2] % 2 == 0 and held + 6 * score_bytes < VMEM_BYTES


def fused_device(sizes, *args):
    (bv, offsets, table, wq, wk, wv, lq, lk, lv, dw) = args
    bytes_count, ctx_count, tp_count = sizes
    rows, channels = bv.shape[0], wq.shape[1]
    shapes = fused_scratch(sizes, rows, table.shape[0], channels, lq.shape[1])
    hops = ctx_count * tp_count // 2
    peers = ctx_count * tp_count
    dma = pltpu.SemaphoreType.DMA
    return pl.pallas_call(
        functools.partial(fused_kernel, *sizes, 3 * rows // 8),
        out_shape=jax.ShapeDtypeStruct((rows, channels), jnp.float32),
        in_specs=[pl.BlockSpec(memory_space=pltpu.VMEM)] * 2
        + [pl.BlockSpec(memory_space=pl.ANY)] * 8,
        out_specs=pl.BlockSpec(memory_space=pltpu.VMEM),
        scratch_shapes=[pltpu.VMEM(shape, kind) for shape, kind in shapes]
        + [
            dma((8,)),
            dma((2,)),
            dma((max(bytes_count - 1, 1),)),
            dma((max(bytes_count - 1, 1),)),
            dma((bytes_count, hops)),
            dma((bytes_count, hops)),
            dma((bytes_count, hops)),
            dma((bytes_count, hops)),
            dma((peers,)),
            dma((peers,)),
        ],
        compiler_params=pltpu.CompilerParams(
            collective_id=0, has_side_effects=True, vmem_limit_bytes=VMEM_BYTES
        ),
        name="fused",
    )(bv.reshape(1, rows), offsets.reshape(1, rows), table, wq, wk, wv, lq, lk, lv, dw).astype(jnp.bfloat16)


def dispatch(sizes, *args):
    rows, vocab = args[0].shape[0], args[2].shape[0]
    channels, latent_columns = args[3].shape[1], args[6].shape[1]
    if fused_fits(sizes, rows, vocab, channels, latent_columns):
        return fused_device(sizes, *args)
    return per_device(*args)


def solution(mesh):
    return jax.shard_map(
        functools.partial(dispatch, tuple(mesh.shape[a] for a in ("bytes", "ctx", "tp"))),
        mesh=mesh,
        in_specs=(
            P(("bytes", "ctx")),
            P(("bytes", "ctx")),
            P(),
            P(None, "tp"),
            P(None, "tp"),
            P(None, "tp"),
            P(None, ("ctx", "tp")),
            P(None, ("ctx", "tp")),
            P(None, ("ctx", "tp")),
            P(("ctx", "tp"), None),
        ),
        out_specs=P(("bytes", "ctx"), "tp"),
        check_vma=False,
    )
```

```python
import functools
import math

import jax
import jax.numpy as jnp
from jax import lax
from jax.experimental import pallas as pl
from jax.experimental.pallas import tpu as pltpu
from jax.sharding import PartitionSpec as P

DB = 1024
HEADS_B = 16
HEAD_L = 128


EPSILON = 1e-06
NEGATIVE = -1e30
FARAWAY = 1 << 30


def from_behind(value, axis, steps):
    count = lax.axis_size(axis)
    first, last = (max(0, -steps), min(count, count - steps))
    return lax.ppermute(value, axis, [(source, source + steps) for source in range(first, last)])


def norm_rows(values):
    values = values.astype(jnp.float32)
    return values * lax.rsqrt(jnp.mean(values * values, axis=-1, keepdims=True) + EPSILON)


def project(inputs, weight):
    return jnp.dot(inputs, weight, preferred_element_type=jnp.float32).astype(jnp.bfloat16)


def byte_project(byte_values_sequence, byte_table, weights):
    onehot = (
        byte_values_sequence[:, None] == jnp.arange(byte_table.shape[0], dtype=jnp.int32)[None, :]
    ).astype(jnp.bfloat16)
    embedded = jnp.dot(onehot, byte_table, preferred_element_type=jnp.float32)
    normed = norm_rows(embedded).astype(jnp.bfloat16)
    return tuple((project(normed, weight) for weight in weights))


def per_device(
    byte_values_sequence,
    offsets,
    byte_table,
    byte_query,
    byte_key,
    byte_value,
    latent_query,
    latent_key,
    latent_value,
    decode_weight,
):
    row_count = byte_values_sequence.shape[0]
    channels = byte_query.shape[1]
    heads_here = HEADS_B * channels // DB
    head_feature_width = channels // heads_here
    ctx_count = lax.axis_size("ctx")
    tp_count = lax.axis_size("tp")
    slot_cap = 3 * row_count // 8
    block_index = lax.axis_index(("bytes", "ctx"))
    byte_window_queries, byte_window_keys, values_b = byte_project(
        byte_values_sequence, byte_table, (byte_query, byte_key, byte_value)
    )
    keys_e, values_e = from_behind((byte_window_keys, values_b), ("bytes", "ctx"), 1)
    keys_w = jnp.concatenate([keys_e, byte_window_keys], axis=0).reshape(
        2 * row_count, heads_here, head_feature_width
    )
    values_w = jnp.concatenate([values_e, values_b], axis=0).reshape(
        2 * row_count, heads_here, head_feature_width
    )
    queries_w = byte_window_queries.reshape(row_count, heads_here, head_feature_width)
    query_pos = jnp.arange(row_count, dtype=jnp.int32)[:, None]
    key_pos = jnp.arange(2 * row_count, dtype=jnp.int32)[None, :]
    allowed_b = (
        (key_pos > query_pos)
        & (key_pos <= query_pos + row_count)
        & ((key_pos >= row_count) | (block_index > 0))
    )
    scores_b = jnp.einsum(
        "qhd,khd->hqk", queries_w, keys_w, preferred_element_type=jnp.float32
    ) / math.sqrt(head_feature_width)
    scores_b = jnp.where(allowed_b[None], scores_b, NEGATIVE)
    highest_b = jnp.max(scores_b, axis=-1, keepdims=True)
    weights_b = jnp.where(allowed_b[None], jnp.exp(scores_b - highest_b), 0.0)
    totals_b = jnp.sum(weights_b, axis=-1)
    blended = jnp.einsum(
        "hqk,khd->qhd", weights_b.astype(jnp.bfloat16), values_w, preferred_element_type=jnp.float32
    )
    encoded = (blended / totals_b.T[:, :, None]).reshape(row_count, channels).astype(jnp.bfloat16)
    starts = (offsets == 0).astype(jnp.int32)
    local_patch = jnp.cumsum(starts) - 1
    members = local_patch[None, :] == jnp.arange(slot_cap, dtype=jnp.int32)[:, None]
    patch_sums = jnp.dot(members.astype(jnp.bfloat16), encoded, preferred_element_type=jnp.float32)
    lengths = jnp.sum(members.astype(jnp.float32), axis=1)
    pooled = (patch_sums / jnp.maximum(lengths, 1.0)[:, None]).astype(jnp.bfloat16)
    gathered, patch_counts = (
        lax.all_gather(pooled, ("ctx", "tp"), axis=0, tiled=True),
        lax.all_gather(local_patch[-1:] + 1, ("ctx", "tp"), axis=0, tiled=True),
    )
    features = gathered.reshape(ctx_count, tp_count, slot_cap, channels).transpose(0, 2, 1, 3)
    features = features.reshape(ctx_count * slot_cap, tp_count * channels)
    patch_counts = patch_counts.reshape(ctx_count, tp_count)[:, 0]
    slot_ids = jnp.arange(slot_cap, dtype=jnp.int32)
    block_ids = lax.axis_index("bytes") * ctx_count + jnp.arange(ctx_count, dtype=jnp.int32)
    positions = jnp.where(
        slot_ids[None, :] < patch_counts[:, None],
        block_ids[:, None] * slot_cap + slot_ids[None, :],
        FARAWAY,
    ).reshape(-1)
    capacity = ctx_count * row_count // 4
    running = jnp.cumsum((positions < FARAWAY).astype(jnp.int32))
    targets = jnp.arange(capacity, dtype=jnp.int32)
    chosen = jnp.minimum(jnp.searchsorted(running, targets + 1), running.shape[0] - 1)
    latent_in = norm_rows(features).astype(jnp.bfloat16)
    queries_l = project(latent_in, latent_query)
    keys_l = project(latent_in, latent_key)
    values_l = project(latent_in, latent_value)
    query_rows = queries_l.shape[0]
    heads_latent = queries_l.shape[1] // HEAD_L
    queries_h = queries_l.reshape(query_rows, heads_latent, HEAD_L)
    initial = (
        jnp.full((heads_latent, query_rows), NEGATIVE, jnp.float32),
        jnp.zeros((heads_latent, query_rows), jnp.float32),
        jnp.zeros((query_rows, heads_latent, HEAD_L), jnp.float32),
    )
    running_state = initial
    keys_p = lax.all_gather(keys_l, "bytes", axis=0, tiled=True)
    values_p = lax.all_gather(values_l, "bytes", axis=0, tiled=True)
    places_p = lax.all_gather(positions, "bytes", axis=0, tiled=True)
    span_rows = keys_p.shape[0]

    def attend_block(state, step_index):
        highest, totals, accumulated = state
        keys_s = lax.dynamic_slice_in_dim(keys_p, step_index * query_rows, query_rows, 0).reshape(
            query_rows, heads_latent, HEAD_L
        )
        values_s = lax.dynamic_slice_in_dim(
            values_p, step_index * query_rows, query_rows, 0
        ).reshape(query_rows, heads_latent, HEAD_L)
        places = lax.dynamic_slice_in_dim(places_p, step_index * query_rows, query_rows, 0)
        attention_scores = jnp.einsum(
            "qhd,khd->hqk", queries_h, keys_s, preferred_element_type=jnp.float32
        ) / math.sqrt(HEAD_L)
        allowed = (places[None, :] <= positions[:, None])[None]
        highest_new = jnp.maximum(
            highest, jnp.max(jnp.where(allowed, attention_scores, NEGATIVE), axis=-1)
        )
        factor = jnp.exp(highest - highest_new)
        weights = jnp.where(allowed, jnp.exp(attention_scores - highest_new[:, :, None]), 0.0)
        totals = totals * factor + jnp.sum(weights, axis=-1)
        mixed_in = jnp.einsum(
            "hqk,khd->qhd",
            weights.astype(jnp.bfloat16),
            values_s,
            preferred_element_type=jnp.float32,
        )
        accumulated = accumulated * factor.T[:, :, None] + mixed_in
        return ((highest_new, totals, accumulated), None)

    running_state, _ = lax.scan(
        attend_block, running_state, jnp.arange(span_rows // query_rows, dtype=jnp.int32)
    )
    highest_l, totals_l, accumulated_l = running_state
    latent_out = (
        (accumulated_l / totals_l.T[:, :, None])
        .reshape(query_rows, heads_latent * HEAD_L)
        .astype(jnp.bfloat16)
    )
    compact = latent_out[chosen]
    shares = lax.psum_scatter(
        jnp.dot(compact, decode_weight, preferred_element_type=jnp.float32).astype(jnp.bfloat16),
        ("ctx", "tp"),
        scatter_dimension=0,
        tiled=True,
    ).astype(jnp.float32)
    summed = lax.all_gather(shares.astype(jnp.bfloat16), ("ctx", "tp"), axis=0, tiled=True).astype(
        shares.dtype
    )
    before = jnp.sum(
        jnp.where(jnp.arange(ctx_count, dtype=jnp.int32) < lax.axis_index("ctx"), patch_counts, 0)
    )
    mine = lax.dynamic_slice_in_dim(summed, lax.axis_index("tp") * channels, channels, 1)
    decoded_bytes = mine[before + local_patch]
    return (encoded.astype(jnp.float32) + decoded_bytes).astype(jnp.bfloat16)


def round_up(value, step):
    return -(-value // step) * step


def fused_kernel(
    bytes_count,
    ctx_count,
    tp_count,
    slot_cap,
    bv_ref,
    off_ref,
    table_hbm,
    wq_hbm,
    wk_hbm,
    wv_hbm,
    lq_hbm,
    lk_hbm,
    lv_hbm,
    dw_hbm,
    out_ref,
    table,
    wb,
    wl,
    dw,
    bv_prev,
    encoded,
    members_ref,
    x_all,
    queries,
    keys,
    values,
    valid,
    bias_ref,
    mixed,
    parts,
    landed,
    load_sems,
    bv_sems,
    z_send,
    z_recv,
    plane_send,
    plane_recv,
    sib_send,
    sib_recv,
    part_send,
    part_recv,
    third_sem,
):
    f32, bf16 = jnp.float32, jnp.bfloat16
    z, c, t = lax.axis_index("bytes"), lax.axis_index("ctx"), lax.axis_index("tp")
    rows = bv_ref.shape[1]
    vocab, width = table.shape
    channels = wb.shape[2]
    slots = x_all.shape[2]
    group = ctx_count * slots
    pairs_y = tp_count // 2
    y, core = t // 2, lax.rem(t, 2)
    mesh_ids = pl.DeviceIdType.MESH

    loads = [
        pltpu.make_async_copy(source, target, load_sems.at[index])
        for index, (source, target) in enumerate(
            (
                (table_hbm, table),
                (wq_hbm, wb.at[0]),
                (wk_hbm, wb.at[1]),
                (wv_hbm, wb.at[2]),
                (lq_hbm, wl.at[0]),
                (lk_hbm, wl.at[1]),
                (lv_hbm, wl.at[2]),
                (dw_hbm, dw),
            )
        )
    ]
    for load in loads:
        load.start()

    block = z * ctx_count + c
    blocks = bytes_count * ctx_count
    after = lax.rem(block + 1, blocks)
    earlier = lax.rem(block + blocks - 1, blocks)
    next_id = (after // ctx_count, lax.rem(after, ctx_count), t)
    prev_id = (earlier // ctx_count, lax.rem(earlier, ctx_count), t)

    hops = [(i, j) for i in range(ctx_count) for j in range(pairs_y)]

    def hop_id(n):
        i, j = hops[n]
        return (z, lax.rem(c + i, ctx_count), lax.rem(y + j, pairs_y) * 2 + core)

    sibling = (z, c, y * 2 + 1 - core)
    barrier = pltpu.get_barrier_semaphore()

    def greet(device):
        pl.semaphore_signal(barrier, inc=1, device_id=device, device_id_type=mesh_ids)

    for device in [sibling] + [hop_id(n) for n in range(1, len(hops))]:
        greet(device)
    expected = len(hops)
    near = [
        ((z + step >= 0) & (z + step < bytes_count), (z + step, c, t))
        for step in (-2, -1, 1, 2)
        if abs(step) < bytes_count
    ]
    near += [(block > 0, prev_id), (block + 1 < blocks, next_id)]
    for present, device in near:
        pl.when(present)(lambda device=device: greet(device))
        expected = expected + jnp.where(present, 1, 0)

    def remote(source, target, send, recv, device):
        return pltpu.make_async_remote_copy(
            src_ref=source,
            dst_ref=target,
            send_sem=send,
            recv_sem=recv,
            device_id=device,
            device_id_type=mesh_ids,
        )

    pl.semaphore_wait(barrier, expected)

    if bytes_count > 3:

        @pl.when((z >= 1) & (z + 2 < bytes_count))
        def _():
            pl.semaphore_signal(
                third_sem, inc=1, device_id=(z - 1, c, t), device_id_type=mesh_ids
            )

    bv_copy = remote(bv_ref, bv_prev, bv_sems.at[0], bv_sems.at[1], next_id)

    @pl.when(block == 0)
    def _():
        bv_prev[...] = jnp.zeros_like(bv_prev)

    pl.when(block + 1 < blocks)(bv_copy.start)

    loads[0].wait()
    table_f = table[...].astype(f32)
    inverse = lax.rsqrt(jnp.mean(table_f * table_f, axis=-1, keepdims=True) + EPSILON)
    normed = (table_f * inverse).astype(bf16)
    tabled = []
    for index in range(3):
        loads[1 + index].wait()
        tabled.append(jnp.dot(normed, wb[index], preferred_element_type=f32).astype(bf16))
    table_q, table_k, table_v = tabled

    starts = (off_ref[...] == 0).astype(f32)
    before = lax.broadcasted_iota(jnp.int32, (rows, rows), 0) <= lax.broadcasted_iota(
        jnp.int32, (rows, rows), 1
    )
    running = jnp.dot(
        jnp.broadcast_to(starts, (16, rows)).astype(bf16),
        before.astype(f32).astype(bf16),
        preferred_element_type=f32,
    )[0:1]
    slot_rows = lax.broadcasted_iota(jnp.int32, (slots, rows), 0).astype(f32)
    members_f = jnp.where(slot_rows == running - 1.0, 1.0, 0.0)
    members = members_f.astype(bf16)
    members_ref[...] = members
    lengths = jnp.sum(members_f, axis=1, keepdims=True)
    patch_count = jnp.sum(starts, axis=1, keepdims=True)

    contract_first = (((0,), (0,)), ((), ()))
    contract_last = (((1,), (1,)), ((), ()))

    def one_hot(ref):
        ids = lax.broadcasted_iota(jnp.int32, (vocab, rows), 0)
        return jnp.where(ids == ref[...], 1.0, 0.0).astype(bf16)

    def pick(hot, source):
        return lax.dot_general(hot, source, contract_first, preferred_element_type=f32).astype(bf16)

    here = one_hot(bv_ref)
    q_b = pick(here, table_q)
    k_here, v_here = pick(here, table_k), pick(here, table_v)
    pl.when(block > 0)(bv_copy.wait_recv)
    past = one_hot(bv_prev)
    k_b = jnp.concatenate([pick(past, table_k), k_here], axis=0)
    v_b = jnp.concatenate([pick(past, table_v), v_here], axis=0)
    query_pos = lax.broadcasted_iota(jnp.int32, (rows, 2 * rows), 0)
    key_pos = lax.broadcasted_iota(jnp.int32, (rows, 2 * rows), 1)
    first_key = jnp.where(block > 0, 0, rows)
    allowed_b = (key_pos > query_pos) & (key_pos <= query_pos + rows) & (key_pos >= first_key)
    bias_b = jnp.where(allowed_b, 0.0, NEGATIVE)
    head_width = DB // HEADS_B
    factor_b = math.log2(math.e) / math.sqrt(head_width)
    per_tile = 128 // head_width
    lane = lax.broadcasted_iota(jnp.int32, (rows, 128), 1)
    for tile in range(channels // 128):
        columns = slice(tile * 128, (tile + 1) * 128)
        q_t, k_t, v_t = q_b[:, columns], k_b[:, columns], v_b[:, columns]
        blended = None
        for head in range(per_tile):
            inside = (lane >= head * head_width) & (lane < (head + 1) * head_width)
            q_h = jnp.where(inside, q_t.astype(f32), 0.0).astype(bf16)
            scores = lax.dot_general(q_h, k_t, contract_last, preferred_element_type=f32) + bias_b
            weights = jnp.exp2((scores - jnp.max(scores, axis=-1, keepdims=True)) * factor_b)
            totals = jnp.sum(weights, axis=-1, keepdims=True)
            mixed_in = jnp.dot(weights.astype(bf16), v_t, preferred_element_type=f32) / totals
            blended = mixed_in if blended is None else jnp.where(inside, mixed_in, blended)
        encoded[:, columns] = blended.astype(bf16)

    sums = jnp.dot(members, encoded[...], preferred_element_type=f32)
    pooled = sums / jnp.maximum(lengths, 1.0)
    slot_ids = lax.broadcasted_iota(jnp.int32, (slots, channels), 0)
    pooled = jnp.where(slot_ids == slot_cap, patch_count, pooled)
    x_all[t, c] = pooled.astype(bf16)

    def piece(tt, d, cc):
        return x_all.at[tt, d * ctx_count + cc]

    def z_copy(d):
        source, step = (0, d) if d <= 3 else (d - 1, 1)
        return remote(
            piece(t, source, c),
            piece(t, d, c),
            z_send.at[d - 1],
            z_recv.at[d - 1],
            (lax.rem(z + step, bytes_count), c, t),
        )

    def z_sends(d):
        return z + d < bytes_count if d <= 3 else (z >= d - 1) & (z + 1 < bytes_count)

    def plane_copy(d, n):
        own = piece(t, d, c)
        return remote(own, own, plane_send.at[d, n], plane_recv.at[d, n], hop_id(n))

    def plane_arrival(d, n):
        i, j = hops[n]
        cc = lax.rem(c + ctx_count - i, ctx_count)
        tt = lax.rem(y + pairs_y - j, pairs_y) * 2 + core
        return piece(tt, d, cc), piece(lax.rem(y + pairs_y - j, pairs_y) * 2 + 1 - core, d, cc)

    def plane_wait(d, n):
        own, _ = plane_arrival(d, n)
        remote(own, own, plane_send.at[d, n], plane_recv.at[d, n], (z, c, t)).wait_recv()

    def sib_copy(d, n):
        own, _ = plane_arrival(d, n)
        return remote(own, own, sib_send.at[d, n], sib_recv.at[d, n], sibling)

    def sib_wait(d, n):
        _, other = plane_arrival(d, n)
        remote(other, other, sib_send.at[d, n], sib_recv.at[d, n], sibling).wait_recv()

    def share(d):
        for n in range(len(hops) - 1, 0, -1):
            plane_copy(d, n).start()
        sib_copy(d, 0).start()

    def forward(d):
        for n in range(1, len(hops)):
            plane_wait(d, n)
            sib_copy(d, n).start()

    if bytes_count > 3:
        pl.when(z + 3 < bytes_count)(lambda: pl.semaphore_wait(third_sem, 1))
    for d in range(min(bytes_count - 1, 3), 0, -1):
        pl.when(z_sends(d))(lambda d=d: z_copy(d).start())
    share(0)
    for d in range(1, bytes_count):

        def pass_on(d=d):
            z_copy(d).wait_recv()
            if d >= 3 and d + 1 < bytes_count:
                pl.when(z_sends(d + 1))(lambda: z_copy(d + 1).start())
            share(d)

        pl.when(z >= d)(pass_on)

    for load in loads[4:]:
        load.wait()

    def latent_rows(d):
        for n in range(len(hops)):
            sib_wait(d, n)
        span = slice(d * ctx_count, (d + 1) * ctx_count)
        features = jnp.concatenate(
            [x_all[tt, span].reshape(group, channels) for tt in range(tp_count)], axis=1
        ).astype(f32)
        scale = lax.rsqrt(jnp.mean(features * features, axis=-1, keepdims=True) + EPSILON)
        latent_in = (features * scale).astype(bf16)
        place = slice(d * group, (d + 1) * group)
        if d == 0:
            queries[...] = jnp.dot(latent_in, wl[0], preferred_element_type=f32).astype(bf16)
        keys[place, :] = jnp.dot(latent_in, wl[1], preferred_element_type=f32).astype(bf16)
        values[place, :] = jnp.dot(latent_in, wl[2], preferred_element_type=f32).astype(bf16)
        slot = lax.broadcasted_iota(jnp.int32, (slots, 128), 0).astype(f32)
        for cc in range(ctx_count):
            count = x_all[0, d * ctx_count + cc, slot_cap : slot_cap + 1, 0:128].astype(f32)
            first = (d * ctx_count + cc) * slots
            valid[first : first + slots, :] = jnp.where(slot < count, 1.0, 0.0).astype(bf16)

    def no_rows(d):
        place = slice(d * group, (d + 1) * group)
        keys[place, :] = jnp.zeros_like(keys[place, :])
        values[place, :] = jnp.zeros_like(values[place, :])
        valid[place, :] = jnp.zeros_like(valid[place, :])

    forward(0)
    for d in range(bytes_count):
        if d + 1 < bytes_count:
            pl.when(z >= d + 1)(lambda d=d: forward(d + 1))
        if d == 0:
            latent_rows(0)
        else:
            pl.when(z >= d)(lambda d=d: latent_rows(d))
            pl.when(z < d)(lambda d=d: no_rows(d))

    span_rows = keys.shape[0]
    exists = lax.dot_general(
        jnp.ones((group, 128), bf16), valid[...], contract_last, preferred_element_type=f32
    )
    row_id = lax.broadcasted_iota(jnp.int32, (group, span_rows), 0)
    col_id = lax.broadcasted_iota(jnp.int32, (group, span_rows), 1)
    bias_ref[...] = jnp.where(
        (exists > 0.5) & ((col_id <= row_id) | (col_id >= group)), 0.0, NEGATIVE
    )
    factor_l = math.log2(math.e) / math.sqrt(HEAD_L)
    for head in range(queries.shape[1] // HEAD_L):
        columns = slice(head * HEAD_L, (head + 1) * HEAD_L)
        scores = (
            lax.dot_general(
                queries[:, columns], keys[:, columns], contract_last, preferred_element_type=f32
            )
            + bias_ref[...]
        )
        weights = jnp.exp2((scores - jnp.max(scores, axis=-1, keepdims=True)) * factor_l)
        totals = jnp.sum(weights, axis=-1, keepdims=True)
        head_out = (
            jnp.dot(weights.astype(bf16), values[:, columns], preferred_element_type=f32) / totals
        ).astype(bf16)
        for cc in range(ctx_count):
            mixed[cc, :, columns] = head_out[cc * slots : (cc + 1) * slots]

    def partial_of(n, parity):
        i, j = hops[n]
        cc, tt = lax.rem(c + i, ctx_count), lax.rem(y + j, pairs_y) * 2 + parity
        columns = pl.ds(pl.multiple_of(tt * channels, channels), channels)
        return jnp.dot(mixed[cc], dw[:, columns], preferred_element_type=f32)

    def part_copy(n, device):
        return remote(parts.at[n], landed.at[n], part_send.at[n], part_recv.at[n], device)

    count = len(hops)
    farthest_first = list(range(count - 1, -1, -1))
    for n in farthest_first:
        parts[n] = partial_of(n, 1 - core).astype(bf16)
        part_copy(n, sibling).start()
    for n in farthest_first:
        decoded = partial_of(n, core)
        part_copy(n, sibling).wait_recv()
        decoded = decoded + landed[n].astype(f32)
        if n:
            parts[count + n] = decoded.astype(bf16)
            part_copy(count + n, hop_id(n)).start()
    for n in farthest_first[:-1]:
        part_copy(count + n, hop_id(n)).wait_recv()
        decoded = decoded + landed[count + n].astype(f32)
    high = decoded.astype(bf16)
    low = (decoded - high.astype(f32)).astype(bf16)
    spread = lax.dot_general(
        members_ref[...], high, contract_first, preferred_element_type=f32
    ) + lax.dot_general(members_ref[...], low, contract_first, preferred_element_type=f32)
    out_ref[...] = encoded[...].astype(f32) + spread

    pl.when(block + 1 < blocks)(bv_copy.wait_send)
    for d in range(1, bytes_count):
        pl.when(z_sends(d))(lambda d=d: z_copy(d).wait_send())

    def shared(d):
        for n in range(len(hops)):
            if n:
                plane_copy(d, n).wait_send()
            sib_copy(d, n).wait_send()

    shared(0)
    for d in range(1, bytes_count):
        pl.when(z >= d)(lambda d=d: shared(d))
    for n in farthest_first:
        part_copy(n, sibling).wait_send()
        if n:
            part_copy(count + n, hop_id(n)).wait_send()


def fused_scratch(sizes, rows, vocab, channels, latent_columns):
    bytes_count, ctx_count, tp_count = sizes
    slots = round_up(3 * rows // 8 + 1, 16)
    group = ctx_count * slots
    span = bytes_count * group
    bf16, f32 = jnp.bfloat16, jnp.float32
    return [
        ((vocab, DB), bf16),
        ((3, DB, channels), bf16),
        ((3, DB, latent_columns), bf16),
        ((latent_columns, DB), bf16),
        ((1, rows), jnp.int32),
        ((rows, channels), bf16),
        ((slots, rows), bf16),
        ((tp_count, bytes_count * ctx_count, slots, channels), bf16),
        ((group, latent_columns), bf16),
        ((span, latent_columns), bf16),
        ((span, latent_columns), bf16),
        ((span, 128), bf16),
        ((group, span), f32),
        ((ctx_count, slots, latent_columns), bf16),
        ((ctx_count * tp_count, slots, channels), bf16),
        ((ctx_count * tp_count, slots, channels), bf16),
    ]


VMEM_BYTES = 60000 * 1024


def fused_fits(sizes, rows, vocab, channels, latent_columns):
    shapes = fused_scratch(sizes, rows, vocab, channels, latent_columns)
    held = sum(math.prod(shape) * jnp.dtype(kind).itemsize for shape, kind in shapes)
    score_bytes = 4 * math.prod(shapes[12][0])
    return sizes[2] % 2 == 0 and held + 6 * score_bytes < VMEM_BYTES


def fused_device(sizes, *args):
    (bv, offsets, table, wq, wk, wv, lq, lk, lv, dw) = args
    bytes_count, ctx_count, tp_count = sizes
    rows, channels = bv.shape[0], wq.shape[1]
    shapes = fused_scratch(sizes, rows, table.shape[0], channels, lq.shape[1])
    hops = ctx_count * tp_count // 2
    peers = ctx_count * tp_count
    dma = pltpu.SemaphoreType.DMA
    return pl.pallas_call(
        functools.partial(fused_kernel, *sizes, 3 * rows // 8),
        out_shape=jax.ShapeDtypeStruct((rows, channels), jnp.float32),
        in_specs=[pl.BlockSpec(memory_space=pltpu.VMEM)] * 2
        + [pl.BlockSpec(memory_space=pl.ANY)] * 8,
        out_specs=pl.BlockSpec(memory_space=pltpu.VMEM),
        scratch_shapes=[pltpu.VMEM(shape, kind) for shape, kind in shapes]
        + [
            dma((8,)),
            dma((2,)),
            dma((max(bytes_count - 1, 1),)),
            dma((max(bytes_count - 1, 1),)),
            dma((bytes_count, hops)),
            dma((bytes_count, hops)),
            dma((bytes_count, hops)),
            dma((bytes_count, hops)),
            dma((peers,)),
            dma((peers,)),
            pltpu.SemaphoreType.REGULAR,
        ],
        compiler_params=pltpu.CompilerParams(
            collective_id=0, has_side_effects=True, vmem_limit_bytes=VMEM_BYTES
        ),
        name="fused",
    )(bv.reshape(1, rows), offsets.reshape(1, rows), table, wq, wk, wv, lq, lk, lv, dw).astype(jnp.bfloat16)


def dispatch(sizes, *args):
    rows, vocab = args[0].shape[0], args[2].shape[0]
    channels, latent_columns = args[3].shape[1], args[6].shape[1]
    if fused_fits(sizes, rows, vocab, channels, latent_columns):
        return fused_device(sizes, *args)
    return per_device(*args)


def solution(mesh):
    return jax.shard_map(
        functools.partial(dispatch, tuple(mesh.shape[a] for a in ("bytes", "ctx", "tp"))),
        mesh=mesh,
        in_specs=(
            P(("bytes", "ctx")),
            P(("bytes", "ctx")),
            P(),
            P(None, "tp"),
            P(None, "tp"),
            P(None, "tp"),
            P(None, ("ctx", "tp")),
            P(None, ("ctx", "tp")),
            P(None, ("ctx", "tp")),
            P(("ctx", "tp"), None),
        ),
        out_specs=P(("bytes", "ctx"), "tp"),
        check_vma=False,
    )
```

```python
import functools
import math

import jax
import jax.numpy as jnp
from jax import lax
from jax.experimental import pallas as pl
from jax.experimental.pallas import tpu as pltpu
from jax.sharding import PartitionSpec as P

DB = 1024
HEADS_B = 16
HEAD_L = 128


EPSILON = 1e-06
NEGATIVE = -1e30
FARAWAY = 1 << 30


def from_behind(value, axis, steps):
    count = lax.axis_size(axis)
    first, last = (max(0, -steps), min(count, count - steps))
    return lax.ppermute(value, axis, [(source, source + steps) for source in range(first, last)])


def norm_rows(values):
    values = values.astype(jnp.float32)
    return values * lax.rsqrt(jnp.mean(values * values, axis=-1, keepdims=True) + EPSILON)


def project(inputs, weight):
    return jnp.dot(inputs, weight, preferred_element_type=jnp.float32).astype(jnp.bfloat16)


def byte_project(byte_values_sequence, byte_table, weights):
    onehot = (
        byte_values_sequence[:, None] == jnp.arange(byte_table.shape[0], dtype=jnp.int32)[None, :]
    ).astype(jnp.bfloat16)
    embedded = jnp.dot(onehot, byte_table, preferred_element_type=jnp.float32)
    normed = norm_rows(embedded).astype(jnp.bfloat16)
    return tuple((project(normed, weight) for weight in weights))


def per_device(
    byte_values_sequence,
    offsets,
    byte_table,
    byte_query,
    byte_key,
    byte_value,
    latent_query,
    latent_key,
    latent_value,
    decode_weight,
):
    row_count = byte_values_sequence.shape[0]
    channels = byte_query.shape[1]
    heads_here = HEADS_B * channels // DB
    head_feature_width = channels // heads_here
    ctx_count = lax.axis_size("ctx")
    tp_count = lax.axis_size("tp")
    slot_cap = 3 * row_count // 8
    block_index = lax.axis_index(("bytes", "ctx"))
    byte_window_queries, byte_window_keys, values_b = byte_project(
        byte_values_sequence, byte_table, (byte_query, byte_key, byte_value)
    )
    keys_e, values_e = from_behind((byte_window_keys, values_b), ("bytes", "ctx"), 1)
    keys_w = jnp.concatenate([keys_e, byte_window_keys], axis=0).reshape(
        2 * row_count, heads_here, head_feature_width
    )
    values_w = jnp.concatenate([values_e, values_b], axis=0).reshape(
        2 * row_count, heads_here, head_feature_width
    )
    queries_w = byte_window_queries.reshape(row_count, heads_here, head_feature_width)
    query_pos = jnp.arange(row_count, dtype=jnp.int32)[:, None]
    key_pos = jnp.arange(2 * row_count, dtype=jnp.int32)[None, :]
    allowed_b = (
        (key_pos > query_pos)
        & (key_pos <= query_pos + row_count)
        & ((key_pos >= row_count) | (block_index > 0))
    )
    scores_b = jnp.einsum(
        "qhd,khd->hqk", queries_w, keys_w, preferred_element_type=jnp.float32
    ) / math.sqrt(head_feature_width)
    scores_b = jnp.where(allowed_b[None], scores_b, NEGATIVE)
    highest_b = jnp.max(scores_b, axis=-1, keepdims=True)
    weights_b = jnp.where(allowed_b[None], jnp.exp(scores_b - highest_b), 0.0)
    totals_b = jnp.sum(weights_b, axis=-1)
    blended = jnp.einsum(
        "hqk,khd->qhd", weights_b.astype(jnp.bfloat16), values_w, preferred_element_type=jnp.float32
    )
    encoded = (blended / totals_b.T[:, :, None]).reshape(row_count, channels).astype(jnp.bfloat16)
    starts = (offsets == 0).astype(jnp.int32)
    local_patch = jnp.cumsum(starts) - 1
    members = local_patch[None, :] == jnp.arange(slot_cap, dtype=jnp.int32)[:, None]
    patch_sums = jnp.dot(members.astype(jnp.bfloat16), encoded, preferred_element_type=jnp.float32)
    lengths = jnp.sum(members.astype(jnp.float32), axis=1)
    pooled = (patch_sums / jnp.maximum(lengths, 1.0)[:, None]).astype(jnp.bfloat16)
    gathered, patch_counts = (
        lax.all_gather(pooled, ("ctx", "tp"), axis=0, tiled=True),
        lax.all_gather(local_patch[-1:] + 1, ("ctx", "tp"), axis=0, tiled=True),
    )
    features = gathered.reshape(ctx_count, tp_count, slot_cap, channels).transpose(0, 2, 1, 3)
    features = features.reshape(ctx_count * slot_cap, tp_count * channels)
    patch_counts = patch_counts.reshape(ctx_count, tp_count)[:, 0]
    slot_ids = jnp.arange(slot_cap, dtype=jnp.int32)
    block_ids = lax.axis_index("bytes") * ctx_count + jnp.arange(ctx_count, dtype=jnp.int32)
    positions = jnp.where(
        slot_ids[None, :] < patch_counts[:, None],
        block_ids[:, None] * slot_cap + slot_ids[None, :],
        FARAWAY,
    ).reshape(-1)
    capacity = ctx_count * row_count // 4
    running = jnp.cumsum((positions < FARAWAY).astype(jnp.int32))
    targets = jnp.arange(capacity, dtype=jnp.int32)
    chosen = jnp.minimum(jnp.searchsorted(running, targets + 1), running.shape[0] - 1)
    latent_in = norm_rows(features).astype(jnp.bfloat16)
    queries_l = project(latent_in, latent_query)
    keys_l = project(latent_in, latent_key)
    values_l = project(latent_in, latent_value)
    query_rows = queries_l.shape[0]
    heads_latent = queries_l.shape[1] // HEAD_L
    queries_h = queries_l.reshape(query_rows, heads_latent, HEAD_L)
    initial = (
        jnp.full((heads_latent, query_rows), NEGATIVE, jnp.float32),
        jnp.zeros((heads_latent, query_rows), jnp.float32),
        jnp.zeros((query_rows, heads_latent, HEAD_L), jnp.float32),
    )
    running_state = initial
    keys_p = lax.all_gather(keys_l, "bytes", axis=0, tiled=True)
    values_p = lax.all_gather(values_l, "bytes", axis=0, tiled=True)
    places_p = lax.all_gather(positions, "bytes", axis=0, tiled=True)
    span_rows = keys_p.shape[0]

    def attend_block(state, step_index):
        highest, totals, accumulated = state
        keys_s = lax.dynamic_slice_in_dim(keys_p, step_index * query_rows, query_rows, 0).reshape(
            query_rows, heads_latent, HEAD_L
        )
        values_s = lax.dynamic_slice_in_dim(
            values_p, step_index * query_rows, query_rows, 0
        ).reshape(query_rows, heads_latent, HEAD_L)
        places = lax.dynamic_slice_in_dim(places_p, step_index * query_rows, query_rows, 0)
        attention_scores = jnp.einsum(
            "qhd,khd->hqk", queries_h, keys_s, preferred_element_type=jnp.float32
        ) / math.sqrt(HEAD_L)
        allowed = (places[None, :] <= positions[:, None])[None]
        highest_new = jnp.maximum(
            highest, jnp.max(jnp.where(allowed, attention_scores, NEGATIVE), axis=-1)
        )
        factor = jnp.exp(highest - highest_new)
        weights = jnp.where(allowed, jnp.exp(attention_scores - highest_new[:, :, None]), 0.0)
        totals = totals * factor + jnp.sum(weights, axis=-1)
        mixed_in = jnp.einsum(
            "hqk,khd->qhd",
            weights.astype(jnp.bfloat16),
            values_s,
            preferred_element_type=jnp.float32,
        )
        accumulated = accumulated * factor.T[:, :, None] + mixed_in
        return ((highest_new, totals, accumulated), None)

    running_state, _ = lax.scan(
        attend_block, running_state, jnp.arange(span_rows // query_rows, dtype=jnp.int32)
    )
    highest_l, totals_l, accumulated_l = running_state
    latent_out = (
        (accumulated_l / totals_l.T[:, :, None])
        .reshape(query_rows, heads_latent * HEAD_L)
        .astype(jnp.bfloat16)
    )
    compact = latent_out[chosen]
    shares = lax.psum_scatter(
        jnp.dot(compact, decode_weight, preferred_element_type=jnp.float32).astype(jnp.bfloat16),
        ("ctx", "tp"),
        scatter_dimension=0,
        tiled=True,
    ).astype(jnp.float32)
    summed = lax.all_gather(shares.astype(jnp.bfloat16), ("ctx", "tp"), axis=0, tiled=True).astype(
        shares.dtype
    )
    before = jnp.sum(
        jnp.where(jnp.arange(ctx_count, dtype=jnp.int32) < lax.axis_index("ctx"), patch_counts, 0)
    )
    mine = lax.dynamic_slice_in_dim(summed, lax.axis_index("tp") * channels, channels, 1)
    decoded_bytes = mine[before + local_patch]
    return (encoded.astype(jnp.float32) + decoded_bytes).astype(jnp.bfloat16)


def round_up(value, step):
    return -(-value // step) * step


def fused_kernel(
    bytes_count,
    ctx_count,
    tp_count,
    slot_cap,
    bv_ref,
    off_ref,
    table_hbm,
    wq_hbm,
    wk_hbm,
    wv_hbm,
    lq_hbm,
    lk_hbm,
    lv_hbm,
    dw_hbm,
    out_ref,
    table,
    wb,
    wl,
    dw,
    bv_prev,
    encoded,
    members_ref,
    x_all,
    queries,
    keys,
    values,
    valid,
    bias_ref,
    mixed,
    parts,
    landed,
    load_sems,
    bv_sems,
    z_send,
    z_recv,
    plane_send,
    plane_recv,
    sib_send,
    sib_recv,
    part_send,
    part_recv,
):
    f32, bf16 = jnp.float32, jnp.bfloat16
    z, c, t = lax.axis_index("bytes"), lax.axis_index("ctx"), lax.axis_index("tp")
    rows = bv_ref.shape[1]
    vocab, width = table.shape
    channels = wb.shape[2]
    slots = x_all.shape[2]
    group = ctx_count * slots
    pairs_y = tp_count // 2
    y, core = t // 2, lax.rem(t, 2)
    mesh_ids = pl.DeviceIdType.MESH

    loads = [
        pltpu.make_async_copy(source, target, load_sems.at[index])
        for index, (source, target) in enumerate(
            (
                (table_hbm, table),
                (wq_hbm, wb.at[0]),
                (wk_hbm, wb.at[1]),
                (wv_hbm, wb.at[2]),
                (lq_hbm, wl.at[0]),
                (lk_hbm, wl.at[1]),
                (lv_hbm, wl.at[2]),
                (dw_hbm, dw),
            )
        )
    ]
    for load in loads:
        load.start()

    block = z * ctx_count + c
    blocks = bytes_count * ctx_count
    after = lax.rem(block + 1, blocks)
    earlier = lax.rem(block + blocks - 1, blocks)
    next_id = (after // ctx_count, lax.rem(after, ctx_count), t)
    prev_id = (earlier // ctx_count, lax.rem(earlier, ctx_count), t)

    hops = [(i, j) for i in range(ctx_count) for j in range(pairs_y)]

    def hop_id(n):
        i, j = hops[n]
        return (z, lax.rem(c + i, ctx_count), lax.rem(y + j, pairs_y) * 2 + core)

    sibling = (z, c, y * 2 + 1 - core)
    barrier = pltpu.get_barrier_semaphore()

    def greet(device):
        pl.semaphore_signal(barrier, inc=1, device_id=device, device_id_type=mesh_ids)

    for device in [sibling] + [hop_id(n) for n in range(1, len(hops))]:
        greet(device)
    expected = len(hops)
    near = [
        ((z + step >= 0) & (z + step < bytes_count), (z + step, c, t))
        for step in (-2, -1, 1, 2)
        if abs(step) < bytes_count
    ]
    near += [(block > 0, prev_id), (block + 1 < blocks, next_id)]
    for present, device in near:
        pl.when(present)(lambda device=device: greet(device))
        expected = expected + jnp.where(present, 1, 0)

    def remote(source, target, send, recv, device):
        return pltpu.make_async_remote_copy(
            src_ref=source,
            dst_ref=target,
            send_sem=send,
            recv_sem=recv,
            device_id=device,
            device_id_type=mesh_ids,
        )

    pl.semaphore_wait(barrier, expected)
    bv_copy = remote(bv_ref, bv_prev, bv_sems.at[0], bv_sems.at[1], next_id)

    @pl.when(block == 0)
    def _():
        bv_prev[...] = jnp.zeros_like(bv_prev)

    pl.when(block + 1 < blocks)(bv_copy.start)

    loads[0].wait()
    table_f = table[...].astype(f32)
    inverse = lax.rsqrt(jnp.mean(table_f * table_f, axis=-1, keepdims=True) + EPSILON)
    normed = (table_f * inverse).astype(bf16)
    tabled = []
    for index in range(3):
        loads[1 + index].wait()
        tabled.append(jnp.dot(normed, wb[index], preferred_element_type=f32).astype(bf16))
    table_q, table_k, table_v = tabled

    starts = (off_ref[...] == 0).astype(f32)
    before = lax.broadcasted_iota(jnp.int32, (rows, rows), 0) <= lax.broadcasted_iota(
        jnp.int32, (rows, rows), 1
    )
    running = jnp.dot(
        jnp.broadcast_to(starts, (16, rows)).astype(bf16),
        before.astype(f32).astype(bf16),
        preferred_element_type=f32,
    )[0:1]
    slot_rows = lax.broadcasted_iota(jnp.int32, (slots, rows), 0).astype(f32)
    members_f = jnp.where(slot_rows == running - 1.0, 1.0, 0.0)
    members = members_f.astype(bf16)
    members_ref[...] = members
    lengths = jnp.sum(members_f, axis=1, keepdims=True)
    patch_count = jnp.sum(starts, axis=1, keepdims=True)

    contract_first = (((0,), (0,)), ((), ()))
    contract_last = (((1,), (1,)), ((), ()))

    def one_hot(ref):
        ids = lax.broadcasted_iota(jnp.int32, (vocab, rows), 0)
        return jnp.where(ids == ref[...], 1.0, 0.0).astype(bf16)

    def pick(hot, source):
        return lax.dot_general(hot, source, contract_first, preferred_element_type=f32).astype(bf16)

    here = one_hot(bv_ref)
    q_b = pick(here, table_q)
    k_here, v_here = pick(here, table_k), pick(here, table_v)
    pl.when(block > 0)(bv_copy.wait_recv)
    past = one_hot(bv_prev)
    k_b = jnp.concatenate([pick(past, table_k), k_here], axis=0)
    v_b = jnp.concatenate([pick(past, table_v), v_here], axis=0)
    query_pos = lax.broadcasted_iota(jnp.int32, (rows, 2 * rows), 0)
    key_pos = lax.broadcasted_iota(jnp.int32, (rows, 2 * rows), 1)
    first_key = jnp.where(block > 0, 0, rows)
    allowed_b = (key_pos > query_pos) & (key_pos <= query_pos + rows) & (key_pos >= first_key)
    bias_b = jnp.where(allowed_b, 0.0, NEGATIVE)
    head_width = DB // HEADS_B
    factor_b = math.log2(math.e) / math.sqrt(head_width)
    per_tile = 128 // head_width
    lane = lax.broadcasted_iota(jnp.int32, (rows, 128), 1)
    for tile in range(channels // 128):
        columns = slice(tile * 128, (tile + 1) * 128)
        q_t, k_t, v_t = q_b[:, columns], k_b[:, columns], v_b[:, columns]
        blended = None
        for head in range(per_tile):
            inside = (lane >= head * head_width) & (lane < (head + 1) * head_width)
            q_h = jnp.where(inside, q_t.astype(f32), 0.0).astype(bf16)
            scores = lax.dot_general(q_h, k_t, contract_last, preferred_element_type=f32) + bias_b
            weights = jnp.exp2((scores - jnp.max(scores, axis=-1, keepdims=True)) * factor_b)
            totals = jnp.sum(weights, axis=-1, keepdims=True)
            mixed_in = jnp.dot(weights.astype(bf16), v_t, preferred_element_type=f32) / totals
            blended = mixed_in if blended is None else jnp.where(inside, mixed_in, blended)
        encoded[:, columns] = blended.astype(bf16)

    sums = jnp.dot(members, encoded[...], preferred_element_type=f32)
    pooled = sums / jnp.maximum(lengths, 1.0)
    slot_ids = lax.broadcasted_iota(jnp.int32, (slots, channels), 0)
    pooled = jnp.where(slot_ids == slot_cap, patch_count, pooled)
    x_all[t, c] = pooled.astype(bf16)

    def piece(tt, d, cc):
        return x_all.at[tt, d * ctx_count + cc]

    def z_copy(d):
        source, step = (0, d) if d <= 2 else (d - 1, 1)
        return remote(
            piece(t, source, c),
            piece(t, d, c),
            z_send.at[d - 1],
            z_recv.at[d - 1],
            (lax.rem(z + step, bytes_count), c, t),
        )

    def z_sends(d):
        return z + d < bytes_count if d <= 2 else (z >= d - 1) & (z + 1 < bytes_count)

    def plane_copy(d, n):
        own = piece(t, d, c)
        return remote(own, own, plane_send.at[d, n], plane_recv.at[d, n], hop_id(n))

    def plane_arrival(d, n):
        i, j = hops[n]
        cc = lax.rem(c + ctx_count - i, ctx_count)
        tt = lax.rem(y + pairs_y - j, pairs_y) * 2 + core
        return piece(tt, d, cc), piece(lax.rem(y + pairs_y - j, pairs_y) * 2 + 1 - core, d, cc)

    def plane_wait(d, n):
        own, _ = plane_arrival(d, n)
        remote(own, own, plane_send.at[d, n], plane_recv.at[d, n], (z, c, t)).wait_recv()

    def sib_copy(d, n):
        own, _ = plane_arrival(d, n)
        return remote(own, own, sib_send.at[d, n], sib_recv.at[d, n], sibling)

    def sib_wait(d, n):
        _, other = plane_arrival(d, n)
        remote(other, other, sib_send.at[d, n], sib_recv.at[d, n], sibling).wait_recv()

    def share(d):
        for n in range(len(hops) - 1, 0, -1):
            plane_copy(d, n).start()
        sib_copy(d, 0).start()

    def forward(d):
        for n in range(1, len(hops)):
            plane_wait(d, n)
            sib_copy(d, n).start()

    for d in range(1, min(bytes_count, 3)):
        pl.when(z_sends(d))(lambda d=d: z_copy(d).start())
    share(0)
    for d in range(1, bytes_count):

        def pass_on(d=d):
            z_copy(d).wait_recv()
            if d >= 2 and d + 1 < bytes_count:
                pl.when(z_sends(d + 1))(lambda: z_copy(d + 1).start())
            share(d)

        pl.when(z >= d)(pass_on)

    for load in loads[4:]:
        load.wait()

    def latent_rows(d):
        for n in range(len(hops)):
            sib_wait(d, n)
        span = slice(d * ctx_count, (d + 1) * ctx_count)
        features = jnp.concatenate(
            [x_all[tt, span].reshape(group, channels) for tt in range(tp_count)], axis=1
        ).astype(f32)
        scale = lax.rsqrt(jnp.mean(features * features, axis=-1, keepdims=True) + EPSILON)
        latent_in = (features * scale).astype(bf16)
        place = slice(d * group, (d + 1) * group)
        if d == 0:
            queries[...] = jnp.dot(latent_in, wl[0], preferred_element_type=f32).astype(bf16)
        keys[place, :] = jnp.dot(latent_in, wl[1], preferred_element_type=f32).astype(bf16)
        values[place, :] = jnp.dot(latent_in, wl[2], preferred_element_type=f32).astype(bf16)
        slot = lax.broadcasted_iota(jnp.int32, (slots, 128), 0).astype(f32)
        for cc in range(ctx_count):
            count = x_all[0, d * ctx_count + cc, slot_cap : slot_cap + 1, 0:128].astype(f32)
            first = (d * ctx_count + cc) * slots
            valid[first : first + slots, :] = jnp.where(slot < count, 1.0, 0.0).astype(bf16)

    def no_rows(d):
        place = slice(d * group, (d + 1) * group)
        keys[place, :] = jnp.zeros_like(keys[place, :])
        values[place, :] = jnp.zeros_like(values[place, :])
        valid[place, :] = jnp.zeros_like(valid[place, :])

    forward(0)
    for d in range(bytes_count):
        if d + 1 < bytes_count:
            pl.when(z >= d + 1)(lambda d=d: forward(d + 1))
        if d == 0:
            latent_rows(0)
        else:
            pl.when(z >= d)(lambda d=d: latent_rows(d))
            pl.when(z < d)(lambda d=d: no_rows(d))

    span_rows = keys.shape[0]
    exists = lax.dot_general(
        jnp.ones((group, 128), bf16), valid[...], contract_last, preferred_element_type=f32
    )
    row_id = lax.broadcasted_iota(jnp.int32, (group, span_rows), 0)
    col_id = lax.broadcasted_iota(jnp.int32, (group, span_rows), 1)
    bias_ref[...] = jnp.where(
        (exists > 0.5) & ((col_id <= row_id) | (col_id >= group)), 0.0, NEGATIVE
    )
    factor_l = math.log2(math.e) / math.sqrt(HEAD_L)
    for head in range(queries.shape[1] // HEAD_L):
        columns = slice(head * HEAD_L, (head + 1) * HEAD_L)
        scores = (
            lax.dot_general(
                queries[:, columns], keys[:, columns], contract_last, preferred_element_type=f32
            )
            + bias_ref[...]
        )
        weights = jnp.exp2((scores - jnp.max(scores, axis=-1, keepdims=True)) * factor_l)
        totals = jnp.sum(weights, axis=-1, keepdims=True)
        head_out = (
            jnp.dot(weights.astype(bf16), values[:, columns], preferred_element_type=f32) / totals
        ).astype(bf16)
        for cc in range(ctx_count):
            mixed[cc, :, columns] = head_out[cc * slots : (cc + 1) * slots]

    def partial_of(n, parity):
        i, j = hops[n]
        cc, tt = lax.rem(c + i, ctx_count), lax.rem(y + j, pairs_y) * 2 + parity
        columns = pl.ds(pl.multiple_of(tt * channels, channels), channels)
        return jnp.dot(mixed[cc], dw[:, columns], preferred_element_type=f32)

    def part_copy(n, device):
        return remote(parts.at[n], landed.at[n], part_send.at[n], part_recv.at[n], device)

    count = len(hops)
    farthest_first = list(range(count - 1, -1, -1))
    for n in farthest_first:
        parts[n] = partial_of(n, 1 - core).astype(bf16)
        part_copy(n, sibling).start()
    for n in farthest_first:
        decoded = partial_of(n, core)
        part_copy(n, sibling).wait_recv()
        decoded = decoded + landed[n].astype(f32)
        if n:
            parts[count + n] = decoded.astype(bf16)
            part_copy(count + n, hop_id(n)).start()
    for n in farthest_first[:-1]:
        part_copy(count + n, hop_id(n)).wait_recv()
        decoded = decoded + landed[count + n].astype(f32)
    high = decoded.astype(bf16)
    low = (decoded - high.astype(f32)).astype(bf16)
    spread = lax.dot_general(
        members_ref[...], high, contract_first, preferred_element_type=f32
    ) + lax.dot_general(members_ref[...], low, contract_first, preferred_element_type=f32)
    out_ref[...] = encoded[...].astype(f32) + spread

    pl.when(block + 1 < blocks)(bv_copy.wait_send)
    for d in range(1, bytes_count):
        pl.when(z_sends(d))(lambda d=d: z_copy(d).wait_send())

    def shared(d):
        for n in range(len(hops)):
            if n:
                plane_copy(d, n).wait_send()
            sib_copy(d, n).wait_send()

    shared(0)
    for d in range(1, bytes_count):
        pl.when(z >= d)(lambda d=d: shared(d))
    for n in farthest_first:
        part_copy(n, sibling).wait_send()
        if n:
            part_copy(count + n, hop_id(n)).wait_send()


def fused_scratch(sizes, rows, vocab, channels, latent_columns):
    bytes_count, ctx_count, tp_count = sizes
    slots = round_up(3 * rows // 8 + 1, 16)
    group = ctx_count * slots
    span = bytes_count * group
    bf16, f32 = jnp.bfloat16, jnp.float32
    return [
        ((vocab, DB), bf16),
        ((3, DB, channels), bf16),
        ((3, DB, latent_columns), bf16),
        ((latent_columns, DB), bf16),
        ((1, rows), jnp.int32),
        ((rows, channels), bf16),
        ((slots, rows), bf16),
        ((tp_count, bytes_count * ctx_count, slots, channels), bf16),
        ((group, latent_columns), bf16),
        ((span, latent_columns), bf16),
        ((span, latent_columns), bf16),
        ((span, 128), bf16),
        ((group, span), f32),
        ((ctx_count, slots, latent_columns), bf16),
        ((ctx_count * tp_count, slots, channels), bf16),
        ((ctx_count * tp_count, slots, channels), bf16),
    ]


VMEM_BYTES = 55000 * 1024


def fused_fits(sizes, rows, vocab, channels, latent_columns):
    shapes = fused_scratch(sizes, rows, vocab, channels, latent_columns)
    held = sum(math.prod(shape) * jnp.dtype(kind).itemsize for shape, kind in shapes)
    score_bytes = 4 * math.prod(shapes[12][0])
    return sizes[2] % 2 == 0 and held + 6 * score_bytes < VMEM_BYTES


def fused_device(sizes, *args):
    (bv, offsets, table, wq, wk, wv, lq, lk, lv, dw) = args
    bytes_count, ctx_count, tp_count = sizes
    rows, channels = bv.shape[0], wq.shape[1]
    shapes = fused_scratch(sizes, rows, table.shape[0], channels, lq.shape[1])
    hops = ctx_count * tp_count // 2
    peers = ctx_count * tp_count
    dma = pltpu.SemaphoreType.DMA
    return pl.pallas_call(
        functools.partial(fused_kernel, *sizes, 3 * rows // 8),
        out_shape=jax.ShapeDtypeStruct((rows, channels), jnp.float32),
        in_specs=[pl.BlockSpec(memory_space=pltpu.VMEM)] * 2
        + [pl.BlockSpec(memory_space=pl.ANY)] * 8,
        out_specs=pl.BlockSpec(memory_space=pltpu.VMEM),
        scratch_shapes=[pltpu.VMEM(shape, kind) for shape, kind in shapes]
        + [
            dma((8,)),
            dma((2,)),
            dma((max(bytes_count - 1, 1),)),
            dma((max(bytes_count - 1, 1),)),
            dma((bytes_count, hops)),
            dma((bytes_count, hops)),
            dma((bytes_count, hops)),
            dma((bytes_count, hops)),
            dma((peers,)),
            dma((peers,)),
        ],
        compiler_params=pltpu.CompilerParams(
            collective_id=0, has_side_effects=True, vmem_limit_bytes=VMEM_BYTES
        ),
        name="fused",
    )(bv.reshape(1, rows), offsets.reshape(1, rows), table, wq, wk, wv, lq, lk, lv, dw).astype(jnp.bfloat16)


def dispatch(sizes, *args):
    rows, vocab = args[0].shape[0], args[2].shape[0]
    channels, latent_columns = args[3].shape[1], args[6].shape[1]
    if fused_fits(sizes, rows, vocab, channels, latent_columns):
        return fused_device(sizes, *args)
    return per_device(*args)


def solution(mesh):
    return jax.shard_map(
        functools.partial(dispatch, tuple(mesh.shape[a] for a in ("bytes", "ctx", "tp"))),
        mesh=mesh,
        in_specs=(
            P(("bytes", "ctx")),
            P(("bytes", "ctx")),
            P(),
            P(None, "tp"),
            P(None, "tp"),
            P(None, "tp"),
            P(None, ("ctx", "tp")),
            P(None, ("ctx", "tp")),
            P(None, ("ctx", "tp")),
            P(("ctx", "tp"), None),
        ),
        out_specs=P(("bytes", "ctx"), "tp"),
        check_vma=False,
    )
```
